512 devices in a mesh: tm: 32 (over y_hi, z, core), space: 16 (over y_lo, x).
Axes of the slice: x: 4, y: 8 (y_hi: 2, y_lo: 4; y = y_hi * 4 + y_lo), z: 8, core: 2. Of those that a mesh axis runs over, the one named last changes fastest.
Arguments:
- iterate: float32 [256, 16, 128, 128], P('tm', 'space'), may hold values from -6 to 6
- forcing: float32 [256, 16, 128, 128], P('tm', 'space'), may hold values from -6 to 6
- start_field: float32 [16, 128, 128], P('space'), may hold values from -6 to 6
- classes: int32 [16, 128, 128], P('space'), may hold values from 0 to 7
- open_mask: int32 [16, 128, 128], P('space'), may hold values 0 or 1
- diffusivity: float32 [8], replicated, may hold values from 0.3 to 3
- drift: float32 [3, 8], replicated, may hold values from -0.9 to 0.9
Outputs:
- residual: float32 [256, 16, 128, 128], P('tm', 'space')
- corrected: float32 [256, 16, 128, 128], P('tm', 'space')
The draws below stay inside these ranges and needn't reach their ends.
All inputs are finite; a program needn't handle non-finite values. No bound on the sum of `open_mask` on one device may be relied on, other than what follows from the above.
Results may differ from the reference program's by a relative error of at most 0.0003.
Values sent between devices are 32-bit elements; how exact they have to be, the bound alone decides.
No kernel may reach another device: no remote copies, remote signals or barrier semaphores. Data moves between devices by JAX's collectives and lax.ppermute only.
A program may use at most 64 MiB of HBM per device.

```python
import math
import jax
import jax.numpy as jnp
from jax import lax

NY = 128
NZ = 128
SWEEPS = 4
NCLASS = 8
NX = 16
L = 256


def place_ends(result, rng, low, top_value):
    dims = result.shape
    index_at = [jax.random.randint(jax.random.fold_in(rng, axis), (), 0, dims[axis]) for axis in range(len(dims))]
    result = result.at[tuple(index_at)].set(low)
    longest = dims.index(max(dims))
    index_at[longest] = (index_at[longest] + 1) % dims[longest]
    return result.at[tuple(index_at)].set(top_value)


def block_scale(key, extent, shards, least, largest):
    factor_of, own = 1.0, jax.random.fold_in(key, 6)
    for axis_at, blocks in shards:
        heights = jnp.exp(jax.random.uniform(jax.random.fold_in(own, axis_at), (blocks,), jnp.float32, least / len(shards), largest / len(shards)))
        factor_of = factor_of * jnp.repeat(heights, extent[axis_at] // blocks).reshape([-1 if axis == axis_at else 1 for axis in range(len(extent))])
    return factor_of


def noise(key, extent, deviation, reach, shards=(), held_as=jnp.bfloat16):
    entries = deviation * jax.random.normal(key, extent, jnp.float32)
    if shards:
        entries = entries * block_scale(key, extent, shards, -0.22, 0.18)
    return jnp.clip(entries, -reach, reach).astype(held_as)


def setup_inputs(seed: int = 0) -> dict:
    key_of = jax.random.split(jax.random.key(seed), 8)
    iterate = noise(key_of[0], (L, NX, NY, NZ), 1.0, 6.0, ((0, 32), (1, 16)), jnp.float32)
    forcing = noise(key_of[1], (L, NX, NY, NZ), 1.0, 6.0, ((0, 32), (1, 16)), jnp.float32)
    start_field = noise(key_of[2], (NX, NY, NZ), 1.0, 6.0, ((0, 16),), jnp.float32)
    classes = place_ends(jax.random.randint(key_of[3], (NX, NY, NZ), 0, NCLASS), jax.random.fold_in(key_of[3], 1), 0, NCLASS - 1).astype(jnp.int32)
    open_mask = place_ends((jax.random.randint(key_of[4], (NX, NY, NZ), 0, 8) < 7).astype(jnp.int32), jax.random.fold_in(key_of[4], 1), 0, 1)
    diffusivity = jnp.clip(jnp.exp(jax.random.uniform(key_of[5], (NCLASS,), jnp.float32, math.log(0.3), math.log(3.0))), 0.3, 3.0)
    drift = jnp.clip(jax.random.uniform(key_of[6], (3, NCLASS), jnp.float32, -0.9, 0.9), -0.9, 0.9)
    return dict(iterate=iterate, forcing=forcing, start_field=start_field, classes=classes, open_mask=open_mask, diffusivity=diffusivity, drift=drift)


ALPHA = 0.1


def step_tables(length):
    index = jnp.arange(length, dtype=jnp.int32)
    folded = (index[:, None] * index[None, :]) % length
    angle = folded.astype(jnp.float32) * (2.0 * math.pi / length)
    cosine = jnp.cos(angle)
    sine = jnp.sin(angle)
    ramp = jnp.exp(index.astype(jnp.float32) * (math.log(ALPHA) / length))
    forward_re = cosine * ramp[None, :]
    forward_im = -sine * ramp[None, :]
    back_re = cosine / (ramp[:, None] * length)
    back_im = -sine / (ramp[:, None] * length)
    root = math.exp(math.log(ALPHA) / length)
    base = index.astype(jnp.float32) * (2.0 * math.pi / length)
    shift_re = 1.0 - root * jnp.cos(base)
    shift_im = root * jnp.sin(base)
    return forward_re, forward_im, back_re, back_im, shift_re, shift_im


def coefficients(classes, open_mask, diffusivity, drift):
    kappa = jnp.zeros(classes.shape, jnp.float32)
    tilt_x = jnp.zeros(classes.shape, jnp.float32)
    tilt_y = jnp.zeros(classes.shape, jnp.float32)
    tilt_z = jnp.zeros(classes.shape, jnp.float32)
    for level in range(diffusivity.shape[0]):
        match = classes == level
        kappa = jnp.where(match, diffusivity[level], kappa)
        tilt_x = jnp.where(match, drift[0, level], tilt_x)
        tilt_y = jnp.where(match, drift[1, level], tilt_y)
        tilt_z = jnp.where(match, drift[2, level], tilt_z)
    weight = open_mask.astype(jnp.float32)
    return weight, kappa, kappa * tilt_x, kappa * tilt_y, kappa * tilt_z


def couple(padded, kappa, flow_x, flow_y, flow_z):
    east = padded[..., 2:, 1:-1, 1:-1]
    west = padded[..., :-2, 1:-1, 1:-1]
    north = padded[..., 1:-1, 2:, 1:-1]
    south = padded[..., 1:-1, :-2, 1:-1]
    upper = padded[..., 1:-1, 1:-1, 2:]
    lower = padded[..., 1:-1, 1:-1, :-2]
    total = kappa * (east + west + north + south + upper + lower)
    return total - flow_x * (east - west) - flow_y * (north - south) - flow_z * (upper - lower)


def solve(source, shift_re, shift_im, weight, kappa, flow_x, flow_y, flow_z, extend):
    real_part = shift_re + 6.0 * kappa
    norm = real_part * real_part + shift_im * shift_im
    inv_re = real_part / norm
    inv_im = -shift_im / norm

    def update(total):
        return jnp.stack([weight * (total[0] * inv_re - total[1] * inv_im),
                          weight * (total[0] * inv_im + total[1] * inv_re)])

    field = update(source)
    for sweep in range(SWEEPS):
        field = update(source + couple(extend(field), kappa, flow_x, flow_y, flow_z))
    return field


def pad_grid(field):
    return jnp.pad(field, ((0, 0), (1, 1), (1, 1), (1, 1)))


def reference(iterate, forcing, start_field, classes, open_mask, diffusivity, drift):
    weight, kappa, flow_x, flow_y, flow_z = coefficients(classes, open_mask, diffusivity, drift)
    previous = jnp.concatenate([start_field[None], iterate[:-1]], axis=0)
    masked = iterate * weight
    applied = weight * (6.0 * kappa * masked - couple(pad_grid(masked), kappa, flow_x, flow_y, flow_z))
    residual = weight * (forcing + previous - iterate) - applied
    forward_re, forward_im, back_re, back_im, shift_re, shift_im = step_tables(L)
    flat = residual.reshape(L, -1)
    spec_re = jnp.dot(forward_re, flat, precision=lax.Precision.HIGHEST).reshape(residual.shape)
    spec_im = jnp.dot(forward_im, flat, precision=lax.Precision.HIGHEST).reshape(residual.shape)
    spectrum = jnp.stack([spec_re, spec_im], axis=1)

    def one(inputs):
        sre, sim, source = inputs
        return solve(source, sre, sim, weight, kappa, flow_x, flow_y, flow_z, pad_grid)

    solved = lax.map(one, (shift_re, shift_im, spectrum))
    part_re = solved[:, 0].reshape(L, -1)
    part_im = solved[:, 1].reshape(L, -1)
    corrected = jnp.dot(back_re, part_re, precision=lax.Precision.HIGHEST) + jnp.dot(back_im, part_im, precision=lax.Precision.HIGHEST)
    return residual, corrected.reshape(residual.shape)
```

```python
import functools
import math

import jax
import jax.numpy as jnp
import numpy as np
from jax import lax
from jax.experimental import pallas as pl
from jax.experimental.pallas import tpu as pltpu
from jax.sharding import Mesh
from jax.sharding import PartitionSpec as P

SWEEPS = 4
ALPHA = 0.1
STEPS = 256
GROUPS = 32
LOCAL = STEPS // GROUPS
NX, NY, NZ = 16, 128, 128
QUARTERS = 4
MEMBERS = GROUPS // QUARTERS
SPAN = NY // QUARTERS
HALO = SWEEPS
WIDE = SPAN + 2 * HALO
WIDE_EACH = WIDE // MEMBERS
EACH = SPAN // MEMBERS
SLOTS = STEPS // 2
CLASSES = 8

AXES = ("yh", "zh", "zl", "core", "yl", "x")
TM = ("yh", "zh", "zl", "core")
SPACE = ("yl", "x")
BLOCK = ("zl", "core", "yl", "x")

VMEM = pl.BlockSpec(memory_space=pltpu.VMEM)
SMEM = pl.BlockSpec(memory_space=pltpu.SMEM)
F32 = jnp.float32


def tables():
    n = np.arange(STEPS, dtype=np.float64)
    k = np.arange(SLOTS, dtype=np.float64)
    ramp = ALPHA ** (n / STEPS)
    angle = 2.0 * np.pi * ((n[None, :] * k[:, None]) % STEPS) / STEPS
    cosine, sine = np.cos(angle), np.sin(angle)
    alternate = np.where(np.arange(STEPS) % 2 == 0, 1.0, -1.0)
    real, imag = cosine.copy(), -sine
    imag[0] = alternate
    forward = np.stack([real, imag], axis=1) * ramp
    forward = forward.reshape(STEPS, STEPS)
    real, imag = 2.0 * cosine, -2.0 * sine
    real[0] = 1.0
    imag[0] = alternate
    back = np.concatenate([real, imag], axis=0) / (ramp * STEPS)
    root = ALPHA ** (1.0 / STEPS)
    base = 2.0 * np.pi * k / STEPS
    first = 1.0 - root * np.cos(base)
    second = first.copy()
    second[0] = 1.0 + root
    turn = root * np.sin(base)
    shift = np.stack([first, second, turn, np.zeros_like(turn)], axis=1)
    return forward.astype(np.float32), back.T.astype(np.float32).copy(), shift.astype(np.float32)


def look_up(classes, kappa_ref, drift_ref):
    kappa = jnp.full(classes.shape, kappa_ref[0], F32)
    flows = [jnp.full(classes.shape, drift_ref[axis, 0], F32) for axis in range(3)]
    for level in range(1, CLASSES):
        match = classes == level
        kappa = jnp.where(match, kappa_ref[level], kappa)
        flows = [jnp.where(match, drift_ref[axis, level], flows[axis]) for axis in range(3)]
    return kappa, [kappa * flow for flow in flows]


def local_terms(masked_ref, forcing_ref, classes_ref, mask_ref, kappa_ref, drift_ref, part_ref, side_ref):
    weight = mask_ref[...].astype(F32)
    kappa, (flow_x, flow_y, flow_z) = look_up(classes_ref[...], kappa_ref, drift_ref)
    row = lax.broadcasted_iota(jnp.int32, (NY, NZ), 0)
    lane = lax.broadcasted_iota(jnp.int32, (NY, NZ), 1)
    side_ref[0] = weight * (kappa - flow_x)
    side_ref[1] = weight * (kappa + flow_x)
    side_ref[2] = weight
    north = jnp.where(row == NY - 1, 0.0, weight * (kappa - flow_y))
    south = jnp.where(row == 0, 0.0, weight * (kappa + flow_y))
    upper = jnp.where(lane == NZ - 1, 0.0, weight * (kappa - flow_z))
    lower = jnp.where(lane == 0, 0.0, weight * (kappa + flow_z))
    middle = 1.0 + 6.0 * kappa
    for n in range(LOCAL):
        here = masked_ref[n]
        total = weight * forcing_ref[n] - middle * here
        total += north * pltpu.roll(here, NY - 1, 0) + south * pltpu.roll(here, 1, 0)
        total += upper * pltpu.roll(here, NZ - 1, 1) + lower * pltpu.roll(here, 1, 1)
        if n:
            total += masked_ref[n - 1]
        part_ref[n] = total


def finish_residual(part_ref, side_ref, east_ref, west_ref, start_ref, arrived_ref, first_ref, residual_ref, sent_ref):
    east, west, weight = side_ref[0], side_ref[1], side_ref[2]
    begins = first_ref[0]
    step_before = weight * jnp.where(begins == 1, start_ref[...], arrived_ref[...])
    for n in range(LOCAL):
        total = part_ref[n] + east * east_ref[n] + west * west_ref[n]
        if n == 0:
            total += step_before
        residual_ref[n] = total
        for quarter in range(QUARTERS):
            low = max(quarter * SPAN - HALO, 0)
            high = min((quarter + 1) * SPAN + HALO, NY)
            at = quarter * WIDE + low - (quarter * SPAN - HALO)
            sent_ref[pl.ds(at * LOCAL + n, high - low, stride=LOCAL), :] = total[low:high]
    outside = jnp.zeros((HALO * LOCAL, NZ), F32)
    sent_ref[0 : HALO * LOCAL, :] = outside
    sent_ref[(QUARTERS * WIDE - HALO) * LOCAL :, :] = outside


def to_frequencies(steps_ref, table_ref, sent_ref):
    fields = [steps_ref[:, row].reshape(STEPS, NZ) for row in range(WIDE_EACH)]
    spectrum = jnp.dot(
        table_ref[...],
        jnp.concatenate(fields, axis=1),
        precision=lax.Precision.HIGHEST,
        preferred_element_type=F32,
    )
    for row in range(WIDE_EACH):
        sent_ref[pl.ds(row, STEPS, stride=WIDE_EACH), :] = spectrum[:, row * NZ : (row + 1) * NZ]


def to_steps(slots_ref, table_ref, sent_ref):
    columns = []
    for row in range(EACH):
        parts = [slots_ref[pl.ds(part * EACH + row, SLOTS, stride=2 * EACH), :] for part in range(2)]
        columns.append(jnp.concatenate(parts, axis=0))
    steps = jnp.dot(
        table_ref[...],
        jnp.concatenate(columns, axis=1),
        precision=lax.Precision.HIGHEST,
        preferred_element_type=F32,
    )
    for row in range(EACH):
        sent_ref[:, row] = steps[:, row * NZ : (row + 1) * NZ].reshape(GROUPS, LOCAL, NZ)


def to_grid(rows_ref, out_ref):
    for n in range(LOCAL):
        out_ref[n] = rows_ref[pl.ds(n, NY, stride=LOCAL), :]


def solve_slot(spectrum_ref, cells_ref, kappa_ref, drift_ref, shift_ref, sent_ref, source, field, coefficient):
    edge = lax.broadcasted_iota(jnp.int32, (NX, NZ), 0)
    lane = lax.broadcasted_iota(jnp.int32, (NX, NZ), 1)
    first, second, turn = shift_ref[0], shift_ref[1], shift_ref[2]
    for member in range(MEMBERS):
        for row in range(WIDE_EACH):
            for part in range(2):
                at = member * NX * 2 * WIDE_EACH + part * WIDE_EACH + row
                source[part, member * WIDE_EACH + row] = spectrum_ref[pl.ds(at, NX, stride=2 * WIDE_EACH), :]

    def prepare(y, carry):
        classes = cells_ref[pl.ds(y, NX, stride=2 * WIDE), :]
        weight = cells_ref[pl.ds(WIDE + y, NX, stride=2 * WIDE), :].astype(F32)
        kappa, (flow_x, flow_y, flow_z) = look_up(classes, kappa_ref, drift_ref)
        coefficient[0, y] = jnp.where(edge == NX - 1, 0.0, kappa - flow_x)
        coefficient[1, y] = jnp.where(edge == 0, 0.0, kappa + flow_x)
        coefficient[2, y] = kappa - flow_y
        coefficient[3, y] = kappa + flow_y
        coefficient[4, y] = jnp.where(lane == NZ - 1, 0.0, kappa - flow_z)
        coefficient[5, y] = jnp.where(lane == 0, 0.0, kappa + flow_z)
        real_first = first + 6.0 * kappa
        real_second = second + 6.0 * kappa
        over_first = weight / (real_first * real_first + turn * turn)
        over_second = weight / (real_second * real_second + turn * turn)
        a, b, c = real_first * over_first, turn * over_first, real_second * over_second
        coefficient[6, y] = a
        coefficient[7, y] = b
        coefficient[8, y] = c
        one, two = source[0, y], source[1, y]
        field[0, 0, y] = a * one + b * two
        field[0, 1, y] = c * two - b * one
        return carry

    lax.fori_loop(0, WIDE, prepare, 0, unroll=2)

    for sweep in range(SWEEPS):
        now, later = sweep % 2, (sweep + 1) % 2

        def row(y, carry):
            totals = []
            for part in range(2):
                here = field[now, part, y]
                total = source[part, y]
                total += coefficient[0, y] * pltpu.roll(here, NX - 1, 0) + coefficient[1, y] * pltpu.roll(here, 1, 0)
                total += coefficient[2, y] * field[now, part, y + 1] + coefficient[3, y] * field[now, part, y - 1]
                total += coefficient[4, y] * pltpu.roll(here, NZ - 1, 1) + coefficient[5, y] * pltpu.roll(here, 1, 1)
                totals.append(total)
            one, two = totals
            a, b, c = coefficient[6, y], coefficient[7, y], coefficient[8, y]
            field[later, 0, y] = a * one + b * two
            field[later, 1, y] = c * two - b * one
            return carry

        lax.fori_loop(sweep + 1, WIDE - 1 - sweep, row, 0, unroll=2)

    for member in range(MEMBERS):
        for row in range(EACH):
            for part in range(2):
                at = member * NX * 2 * EACH + part * EACH + row
                sent_ref[pl.ds(at, NX, stride=2 * EACH), :] = field[SWEEPS % 2, part, HALO + member * EACH + row]


def call(kernel, out_shape, in_specs, scratch=(), flops=1_000_000, moved=2_000_000):
    return pl.pallas_call(
        kernel,
        out_shape=out_shape,
        in_specs=in_specs,
        out_specs=jax.tree.map(lambda _: VMEM, out_shape),
        scratch_shapes=scratch,
        cost_estimate=pl.CostEstimate(flops=flops, bytes_accessed=moved, transcendentals=0),
    )


def shape(*dims):
    return jax.ShapeDtypeStruct(dims, F32)


def exchange(value, axes):
    return lax.all_to_all(value, axes, split_axis=0, concat_axis=0, tiled=True)


def local(iterate, forcing, start_field, classes, open_mask, diffusivity, drift):
    forward, back, shift = tables()
    iterate = iterate.reshape(LOCAL, NY, NZ)
    forcing = forcing.reshape(LOCAL, NY, NZ)
    start_field = start_field.reshape(NY, NZ)
    classes = classes.reshape(NY, NZ)
    open_mask = open_mask.reshape(NY, NZ)

    masked = iterate * open_mask.astype(F32)
    up = [(i, i + 1) for i in range(NX - 1)]
    down = [(j, i) for i, j in up]
    west = lax.ppermute(masked, SPACE, up)
    east = lax.ppermute(masked, SPACE, down)
    arrived = lax.ppermute(masked[LOCAL - 1], TM, [(i, i + 1) for i in range(GROUPS - 1)])

    quarter = lax.axis_index(("yh", "zh"))
    pad = ((HALO, HALO), (0, 0))
    cells = jnp.concatenate(
        [
            lax.dynamic_slice_in_dim(jnp.pad(plane, pad), quarter * SPAN, WIDE, 0)
            for plane in (classes, open_mask)
        ]
    )
    cells = jnp.broadcast_to(cells[None], (NX, 2 * WIDE, NZ)).reshape(NX * 2 * WIDE, NZ)
    cells = exchange(cells, SPACE)

    part, side = call(
        local_terms,
        (shape(LOCAL, NY, NZ), shape(3, NY, NZ)),
        [VMEM] * 4 + [SMEM] * 2,
    )(masked, forcing, classes, open_mask, diffusivity, drift)
    first = (lax.axis_index(TM) == 0).astype(jnp.int32).reshape(1)
    residual, sent = call(
        finish_residual,
        (shape(LOCAL, NY, NZ), shape(QUARTERS * WIDE * LOCAL, NZ)),
        [VMEM] * 6 + [SMEM],
    )(part, side, east, west, start_field, arrived, first)

    steps = exchange(sent, TM).reshape(GROUPS, WIDE_EACH, LOCAL, NZ)
    sent = call(to_frequencies, shape(SLOTS * 2 * WIDE_EACH, NZ), [VMEM] * 2)(steps, jnp.asarray(forward))
    spectrum = exchange(sent, BLOCK)
    mine = lax.dynamic_slice_in_dim(jnp.asarray(shift), lax.axis_index(BLOCK), 1, 0).reshape(4)
    sent = call(
        solve_slot,
        shape(SLOTS * 2 * EACH, NZ),
        [VMEM] * 2 + [SMEM] * 3,
        scratch=[
            pltpu.VMEM((2, WIDE, NX, NZ), F32),
            pltpu.VMEM((2, 2, WIDE, NX, NZ), F32),
            pltpu.VMEM((9, WIDE, NX, NZ), F32),
        ],
    )(spectrum, cells, diffusivity, drift, mine)
    solved = exchange(sent, BLOCK)
    sent = call(to_steps, shape(GROUPS, EACH, LOCAL, NZ), [VMEM] * 2)(solved, jnp.asarray(back))
    rows = exchange(sent.reshape(GROUPS * EACH * LOCAL, NZ), TM)
    corrected = call(to_grid, shape(LOCAL, NY, NZ), [VMEM])(rows)
    grid = (LOCAL, 1, NY, NZ)
    return residual.reshape(grid), corrected.reshape(grid)


def solution(mesh):
    fine = Mesh(mesh.devices.reshape(2, 2, 4, 2, 4, 4), AXES)
    big = P(TM, SPACE, None, None)
    plane = P(SPACE, None, None)
    return jax.shard_map(
        local,
        mesh=fine,
        in_specs=(big, big, plane, plane, plane, P(), P()),
        out_specs=(big, big),
        check_vma=False,
    )
```

```python
import functools
import math

import jax
import jax.numpy as jnp
import numpy as np
from jax import lax
from jax.experimental import pallas as pl
from jax.experimental.pallas import tpu as pltpu
from jax.sharding import Mesh
from jax.sharding import PartitionSpec as P

SWEEPS = 4
ALPHA = 0.1
STEPS = 256
GROUPS = 32
LOCAL = STEPS // GROUPS
NX, NY, NZ = 16, 128, 128
QUARTERS = 4
MEMBERS = GROUPS // QUARTERS
SPAN = NY // QUARTERS
HALO = SWEEPS
WIDE = SPAN + 2 * HALO
WIDE_EACH = WIDE // MEMBERS
EACH = SPAN // MEMBERS
SLOTS = STEPS // 2
CLASSES = 8
SOLID = CLASSES
SENT = 16

AXES = ("yh", "zh", "zl", "core", "yl", "x")
TM = ("yh", "zh", "zl", "core")
SPACE = ("yl", "x")
BLOCK = ("zl", "core", "yl", "x")

GRANT = 24 << 20
VMEM = pl.BlockSpec(memory_space=pltpu.VMEM)
SMEM = pl.BlockSpec(memory_space=pltpu.SMEM)
F32 = jnp.float32


def tables():
    n = np.arange(STEPS, dtype=np.float64)
    k = np.arange(SLOTS, dtype=np.float64)
    ramp = ALPHA ** (n / STEPS)
    angle = 2.0 * np.pi * ((n[None, :] * k[:, None]) % STEPS) / STEPS
    cosine, sine = np.cos(angle), np.sin(angle)
    alternate = np.where(np.arange(STEPS) % 2 == 0, 1.0, -1.0)
    real, imag = cosine.copy(), -sine
    imag[0] = alternate
    forward = np.concatenate([real, imag], axis=0) * ramp
    real, imag = 2.0 * cosine, -2.0 * sine
    real[0] = 1.0
    imag[0] = alternate
    back = np.concatenate([real, imag], axis=0) / (ramp * STEPS)
    root = ALPHA ** (1.0 / STEPS)
    base = 2.0 * np.pi * k / STEPS
    first = 1.0 - root * np.cos(base)
    second = first.copy()
    second[0] = 1.0 + root
    turn = root * np.sin(base)
    shift = np.stack([first, second, turn, np.zeros_like(turn)], axis=1)
    return forward.astype(np.float32), back.T.astype(np.float32).copy(), shift.astype(np.float32)


def look_up(classes, kappa_ref, drift_ref):
    kappa = jnp.full(classes.shape, kappa_ref[0], F32)
    flows = [jnp.full(classes.shape, drift_ref[axis, 0], F32) for axis in range(3)]
    for level in range(1, CLASSES):
        match = classes == level
        kappa = jnp.where(match, kappa_ref[level], kappa)
        flows = [jnp.where(match, drift_ref[axis, level], flows[axis]) for axis in range(3)]
    return kappa, [kappa * flow for flow in flows]


def local_terms(masked_ref, forcing_ref, classes_ref, mask_ref, kappa_ref, drift_ref, part_ref, side_ref):
    weight = mask_ref[...].astype(F32)
    kappa, (flow_x, flow_y, flow_z) = look_up(classes_ref[...], kappa_ref, drift_ref)
    row = lax.broadcasted_iota(jnp.int32, (NY, NZ), 0)
    lane = lax.broadcasted_iota(jnp.int32, (NY, NZ), 1)
    side_ref[0] = weight * (kappa - flow_x)
    side_ref[1] = weight * (kappa + flow_x)
    side_ref[2] = weight
    north = jnp.where(row == NY - 1, 0.0, weight * (kappa - flow_y))
    south = jnp.where(row == 0, 0.0, weight * (kappa + flow_y))
    upper = jnp.where(lane == NZ - 1, 0.0, weight * (kappa - flow_z))
    lower = jnp.where(lane == 0, 0.0, weight * (kappa + flow_z))
    middle = 1.0 + 6.0 * kappa
    for n in range(LOCAL):
        here = masked_ref[n]
        total = weight * forcing_ref[n] - middle * here
        total += north * pltpu.roll(here, NY - 1, 0) + south * pltpu.roll(here, 1, 0)
        total += upper * pltpu.roll(here, NZ - 1, 1) + lower * pltpu.roll(here, 1, 1)
        if n:
            total += masked_ref[n - 1]
        part_ref[n] = total


def finish_residual(part_ref, side_ref, east_ref, west_ref, start_ref, arrived_ref, first_ref, residual_ref, sent_ref):
    east, west, weight = side_ref[0], side_ref[1], side_ref[2]
    begins = first_ref[0]
    step_before = weight * jnp.where(begins == 1, start_ref[...], arrived_ref[...])
    for n in range(LOCAL):
        total = part_ref[n] + east * east_ref[n] + west * west_ref[n]
        if n == 0:
            total += step_before
        residual_ref[n] = total
        for quarter in range(QUARTERS):
            low = max(quarter * SPAN - HALO, 0)
            high = min((quarter + 1) * SPAN + HALO, NY)
            at = quarter * WIDE + low - (quarter * SPAN - HALO)
            sent_ref[pl.ds(at * LOCAL + n, high - low, stride=LOCAL), :] = total[low:high]
    outside = jnp.zeros((HALO * LOCAL, NZ), F32)
    sent_ref[0 : HALO * LOCAL, :] = outside
    sent_ref[(QUARTERS * WIDE - HALO) * LOCAL :, :] = outside


def to_frequencies(steps_ref, cells_ref, table_ref, sent_ref):
    fields = [steps_ref[:, row].reshape(STEPS, NZ) for row in range(WIDE_EACH)]
    spectrum = jnp.dot(
        table_ref[...],
        jnp.concatenate(fields, axis=1),
        precision=lax.Precision.HIGHEST,
        preferred_element_type=F32,
    )
    for row in range(WIDE_EACH):
        columns = spectrum[:, row * NZ : (row + 1) * NZ]
        for part in range(2):
            rows = columns[part * SLOTS : (part + 1) * SLOTS]
            sent_ref[pl.ds(part * WIDE_EACH + row, SLOTS, stride=SENT), :] = rows
        cells = jnp.broadcast_to(cells_ref[row : row + 1, :], (SLOTS, NZ))
        sent_ref[pl.ds(2 * WIDE_EACH + row, SLOTS, stride=SENT), :] = cells
    for row in range(3 * WIDE_EACH, SENT):
        sent_ref[pl.ds(row, SLOTS, stride=SENT), :] = jnp.zeros((SLOTS, NZ), F32)


def to_steps(slots_ref, table_ref, sent_ref):
    columns = []
    for row in range(EACH):
        parts = [slots_ref[pl.ds(part * EACH + row, SLOTS, stride=2 * EACH), :] for part in range(2)]
        columns.append(jnp.concatenate(parts, axis=0))
    steps = jnp.dot(
        table_ref[...],
        jnp.concatenate(columns, axis=1),
        precision=lax.Precision.HIGHEST,
        preferred_element_type=F32,
    )
    for row in range(EACH):
        sent_ref[:, row] = steps[:, row * NZ : (row + 1) * NZ].reshape(GROUPS, LOCAL, NZ)


def to_grid(rows_ref, out_ref):
    for n in range(LOCAL):
        out_ref[n] = rows_ref[pl.ds(n, NY, stride=LOCAL), :]


def solve_slot(spectrum_ref, kappa_ref, drift_ref, shift_ref, sent_ref, source, cells, field, coefficient):
    edge = lax.broadcasted_iota(jnp.int32, (NX, NZ), 0)
    lane = lax.broadcasted_iota(jnp.int32, (NX, NZ), 1)
    first, second, turn = shift_ref[0], shift_ref[1], shift_ref[2]
    for member in range(MEMBERS):
        for row in range(WIDE_EACH):
            at = member * NX * SENT + row
            for part in range(2):
                source[part, member * WIDE_EACH + row] = spectrum_ref[pl.ds(at + part * WIDE_EACH, NX, stride=SENT), :]
            cells[member * WIDE_EACH + row] = spectrum_ref[pl.ds(at + 2 * WIDE_EACH, NX, stride=SENT), :]

    def prepare(y, carry):
        classes = cells[y].astype(jnp.int32)
        weight = jnp.where(classes == SOLID, 0.0, 1.0)
        kappa, (flow_x, flow_y, flow_z) = look_up(classes, kappa_ref, drift_ref)
        coefficient[0, y] = jnp.where(edge == NX - 1, 0.0, kappa - flow_x)
        coefficient[1, y] = jnp.where(edge == 0, 0.0, kappa + flow_x)
        coefficient[2, y] = kappa - flow_y
        coefficient[3, y] = kappa + flow_y
        coefficient[4, y] = jnp.where(lane == NZ - 1, 0.0, kappa - flow_z)
        coefficient[5, y] = jnp.where(lane == 0, 0.0, kappa + flow_z)
        real_first = first + 6.0 * kappa
        real_second = second + 6.0 * kappa
        over_first = weight / (real_first * real_first + turn * turn)
        over_second = weight / (real_second * real_second + turn * turn)
        a, b, c = real_first * over_first, turn * over_first, real_second * over_second
        coefficient[6, y] = a
        coefficient[7, y] = b
        coefficient[8, y] = c
        one, two = source[0, y], source[1, y]
        field[0, 0, y] = a * one + b * two
        field[0, 1, y] = c * two - b * one
        return carry

    lax.fori_loop(0, WIDE, prepare, 0, unroll=2)

    for sweep in range(SWEEPS):
        now, later = sweep % 2, (sweep + 1) % 2

        def row(y, carry):
            totals = []
            for part in range(2):
                here = field[now, part, y]
                total = source[part, y]
                total += coefficient[0, y] * pltpu.roll(here, NX - 1, 0) + coefficient[1, y] * pltpu.roll(here, 1, 0)
                total += coefficient[2, y] * field[now, part, y + 1] + coefficient[3, y] * field[now, part, y - 1]
                total += coefficient[4, y] * pltpu.roll(here, NZ - 1, 1) + coefficient[5, y] * pltpu.roll(here, 1, 1)
                totals.append(total)
            one, two = totals
            a, b, c = coefficient[6, y], coefficient[7, y], coefficient[8, y]
            field[later, 0, y] = a * one + b * two
            field[later, 1, y] = c * two - b * one
            return carry

        lax.fori_loop(sweep + 1, WIDE - 1 - sweep, row, 0, unroll=2)

    for member in range(MEMBERS):
        for row in range(EACH):
            for part in range(2):
                at = member * NX * 2 * EACH + part * EACH + row
                sent_ref[pl.ds(at, NX, stride=2 * EACH), :] = field[SWEEPS % 2, part, HALO + member * EACH + row]


def call(kernel, out_shape, in_specs, scratch=(), flops=1_000_000, moved=2_000_000):
    return pl.pallas_call(
        kernel,
        out_shape=out_shape,
        in_specs=in_specs,
        out_specs=jax.tree.map(lambda _: VMEM, out_shape),
        scratch_shapes=scratch,
        cost_estimate=pl.CostEstimate(flops=flops, bytes_accessed=moved, transcendentals=0),
        compiler_params=pltpu.CompilerParams(vmem_limit_bytes=GRANT),
    )


def shape(*dims):
    return jax.ShapeDtypeStruct(dims, F32)


def exchange(value, axes):
    return lax.all_to_all(value, axes, split_axis=0, concat_axis=0, tiled=True)


def local(iterate, forcing, start_field, classes, open_mask, diffusivity, drift):
    forward, back, shift = tables()
    iterate = iterate.reshape(LOCAL, NY, NZ)
    forcing = forcing.reshape(LOCAL, NY, NZ)
    start_field = start_field.reshape(NY, NZ)
    classes = classes.reshape(NY, NZ)
    open_mask = open_mask.reshape(NY, NZ)

    masked = iterate * open_mask.astype(F32)
    up = [(i, i + 1) for i in range(NX - 1)]
    down = [(j, i) for i, j in up]
    west = lax.ppermute(masked, SPACE, up)
    east = lax.ppermute(masked, SPACE, down)
    arrived = lax.ppermute(masked[LOCAL - 1], TM, [(i, i + 1) for i in range(GROUPS - 1)])

    cells = jnp.pad(jnp.where(open_mask == 1, classes, SOLID), ((HALO, HALO), (0, 0)), constant_values=SOLID)
    row = lax.axis_index(("yh", "zh")) * SPAN + lax.axis_index(("zl", "core")) * WIDE_EACH
    cells = lax.dynamic_slice_in_dim(cells, row, WIDE_EACH, 0).astype(F32)

    part, side = call(
        local_terms,
        (shape(LOCAL, NY, NZ), shape(3, NY, NZ)),
        [VMEM] * 4 + [SMEM] * 2,
    )(masked, forcing, classes, open_mask, diffusivity, drift)
    first = (lax.axis_index(TM) == 0).astype(jnp.int32).reshape(1)
    residual, sent = call(
        finish_residual,
        (shape(LOCAL, NY, NZ), shape(QUARTERS * WIDE * LOCAL, NZ)),
        [VMEM] * 6 + [SMEM],
    )(part, side, east, west, start_field, arrived, first)

    steps = exchange(sent, TM).reshape(GROUPS, WIDE_EACH, LOCAL, NZ)
    sent = call(to_frequencies, shape(SLOTS * SENT, NZ), [VMEM] * 3)(steps, cells, jnp.asarray(forward))
    spectrum = exchange(sent, BLOCK)
    mine = lax.dynamic_slice_in_dim(jnp.asarray(shift), lax.axis_index(BLOCK), 1, 0).reshape(4)
    sent = call(
        solve_slot,
        shape(SLOTS * 2 * EACH, NZ),
        [VMEM] + [SMEM] * 3,
        scratch=[
            pltpu.VMEM((2, WIDE, NX, NZ), F32),
            pltpu.VMEM((WIDE, NX, NZ), F32),
            pltpu.VMEM((2, 2, WIDE, NX, NZ), F32),
            pltpu.VMEM((9, WIDE, NX, NZ), F32),
        ],
    )(spectrum, diffusivity, drift, mine)
    solved = exchange(sent, BLOCK)
    sent = call(to_steps, shape(GROUPS, EACH, LOCAL, NZ), [VMEM] * 2)(solved, jnp.asarray(back))
    rows = exchange(sent.reshape(GROUPS * EACH * LOCAL, NZ), TM)
    corrected = call(to_grid, shape(LOCAL, NY, NZ), [VMEM])(rows)
    grid = (LOCAL, 1, NY, NZ)
    return residual.reshape(grid), corrected.reshape(grid)


def solution(mesh):
    fine = Mesh(mesh.devices.reshape(2, 2, 4, 2, 4, 4), AXES)
    big = P(TM, SPACE, None, None)
    plane = P(SPACE, None, None)
    return jax.shard_map(
        local,
        mesh=fine,
        in_specs=(big, big, plane, plane, plane, P(), P()),
        out_specs=(big, big),
        check_vma=False,
    )
```

```python
import jax
import jax.numpy as jnp
import numpy as np
from jax import lax
from jax.experimental import pallas as pl
from jax.experimental.pallas import tpu as pltpu
from jax.sharding import Mesh
from jax.sharding import PartitionSpec as P


SWEEPS = 4
ALPHA = 0.1
STEPS = 256
GROUPS = 32
LOCAL = STEPS // GROUPS
NX, NY, NZ = 16, 128, 128
QUARTERS = 4
MEMBERS = GROUPS // QUARTERS
SPAN = NY // QUARTERS
HALO = SWEEPS
WIDE = SPAN + 2 * HALO
WIDE_EACH = WIDE // MEMBERS
EACH = SPAN // MEMBERS
SLOTS = STEPS // 2
CLASSES = 8
SOLID = CLASSES

AXES = ("yh", "zh", "zl", "core", "yl", "x")
TM = ("yh", "zh", "zl", "core")
SPACE = ("yl", "x")
BLOCK = ("zl", "core", "yl", "x")

GRANT = 24 << 20
VMEM = pl.BlockSpec(memory_space=pltpu.VMEM)
SMEM = pl.BlockSpec(memory_space=pltpu.SMEM)
F32 = jnp.float32


def tables():
    n = np.arange(STEPS, dtype=np.float64)
    k = np.arange(SLOTS, dtype=np.float64)
    ramp = ALPHA ** (n / STEPS)
    angle = 2.0 * np.pi * ((n[None, :] * k[:, None]) % STEPS) / STEPS
    cosine, sine = np.cos(angle), np.sin(angle)
    alternate = np.where(np.arange(STEPS) % 2 == 0, 1.0, -1.0)
    real, imag = cosine.copy(), -sine
    imag[0] = alternate
    forward = np.concatenate([real, imag], axis=0) * ramp
    real, imag = 2.0 * cosine, -2.0 * sine
    real[0] = 1.0
    imag[0] = alternate
    back = np.concatenate([real, imag], axis=0) / (ramp * STEPS)
    root = ALPHA ** (1.0 / STEPS)
    base = 2.0 * np.pi * k / STEPS
    first = 1.0 - root * np.cos(base)
    second = first.copy()
    second[0] = 1.0 + root
    turn = root * np.sin(base)
    shift = np.stack([first, second, turn, np.zeros_like(turn)], axis=1)
    return forward.astype(np.float32), back.T.astype(np.float32).copy(), shift.astype(np.float32)


def look_up(classes, kappa_ref, drift_ref):
    kappa = jnp.full(classes.shape, kappa_ref[0], F32)
    flows = [jnp.full(classes.shape, drift_ref[axis, 0], F32) for axis in range(3)]
    for level in range(1, CLASSES):
        match = classes == level
        kappa = jnp.where(match, kappa_ref[level], kappa)
        flows = [jnp.where(match, drift_ref[axis, level], flows[axis]) for axis in range(3)]
    return kappa, [kappa * flow for flow in flows]


def local_terms(masked_ref, forcing_ref, classes_ref, mask_ref, kappa_ref, drift_ref, part_ref, side_ref):
    weight = mask_ref[...].astype(F32)
    kappa, (flow_x, flow_y, flow_z) = look_up(classes_ref[...], kappa_ref, drift_ref)
    row = lax.broadcasted_iota(jnp.int32, (NY, NZ), 0)
    lane = lax.broadcasted_iota(jnp.int32, (NY, NZ), 1)
    side_ref[0] = weight * (kappa - flow_x)
    side_ref[1] = weight * (kappa + flow_x)
    side_ref[2] = weight
    north = jnp.where(row == NY - 1, 0.0, weight * (kappa - flow_y))
    south = jnp.where(row == 0, 0.0, weight * (kappa + flow_y))
    upper = jnp.where(lane == NZ - 1, 0.0, weight * (kappa - flow_z))
    lower = jnp.where(lane == 0, 0.0, weight * (kappa + flow_z))
    middle = 1.0 + 6.0 * kappa
    for n in range(LOCAL):
        here = masked_ref[n]
        total = weight * forcing_ref[n] - middle * here
        total += north * pltpu.roll(here, NY - 1, 0) + south * pltpu.roll(here, 1, 0)
        total += upper * pltpu.roll(here, NZ - 1, 1) + lower * pltpu.roll(here, 1, 1)
        if n:
            total += masked_ref[n - 1]
        part_ref[n] = total


def finish_residual(part_ref, side_ref, east_ref, west_ref, start_ref, arrived_ref, first_ref, residual_ref, sent_ref):
    east, west, weight = side_ref[0], side_ref[1], side_ref[2]
    begins = first_ref[0]
    step_before = weight * jnp.where(begins == 1, start_ref[...], arrived_ref[...])
    for n in range(LOCAL):
        total = part_ref[n] + east * east_ref[n] + west * west_ref[n]
        if n == 0:
            total += step_before
        residual_ref[n] = total
        for quarter in range(QUARTERS):
            low = max(quarter * SPAN - HALO, 0)
            high = min((quarter + 1) * SPAN + HALO, NY)
            at = quarter * WIDE + low - (quarter * SPAN - HALO)
            sent_ref[pl.ds(at * LOCAL + n, high - low, stride=LOCAL), :] = total[low:high]
    outside = jnp.zeros((HALO * LOCAL, NZ), F32)
    sent_ref[0 : HALO * LOCAL, :] = outside
    sent_ref[(QUARTERS * WIDE - HALO) * LOCAL :, :] = outside


def to_frequencies(steps_ref, table_ref, sent_ref):
    fields = [steps_ref[:, row].reshape(STEPS, NZ) for row in range(WIDE_EACH)]
    spectrum = jnp.dot(
        table_ref[...],
        jnp.concatenate(fields, axis=1),
        precision=lax.Precision.HIGHEST,
        preferred_element_type=F32,
    )
    for row in range(WIDE_EACH):
        columns = spectrum[:, row * NZ : (row + 1) * NZ]
        for part in range(2):
            rows = columns[part * SLOTS : (part + 1) * SLOTS]
            sent_ref[pl.ds(part * WIDE_EACH + row, SLOTS, stride=2 * WIDE_EACH), :] = rows


def to_steps(slots_ref, table_ref, sent_ref):
    columns = []
    for row in range(EACH):
        parts = [slots_ref[pl.ds(part * EACH + row, SLOTS, stride=2 * EACH), :] for part in range(2)]
        columns.append(jnp.concatenate(parts, axis=0))
    steps = jnp.dot(
        table_ref[...],
        jnp.concatenate(columns, axis=1),
        precision=lax.Precision.HIGHEST,
        preferred_element_type=F32,
    )
    for row in range(EACH):
        sent_ref[:, row] = steps[:, row * NZ : (row + 1) * NZ].reshape(GROUPS, LOCAL, NZ)


def to_grid(rows_ref, out_ref):
    for n in range(LOCAL):
        out_ref[n] = rows_ref[pl.ds(n, NY, stride=LOCAL), :]


def solve_slot(spectrum_ref, cells_ref, kappa_ref, drift_ref, shift_ref, sent_ref, source, field, coefficient):
    edge = lax.broadcasted_iota(jnp.int32, (NX, NZ), 0)
    lane = lax.broadcasted_iota(jnp.int32, (NX, NZ), 1)
    first, second, turn = shift_ref[0], shift_ref[1], shift_ref[2]
    for member in range(MEMBERS):
        for row in range(WIDE_EACH):
            at = member * NX * 2 * WIDE_EACH + row
            for part in range(2):
                rows = pl.ds(at + part * WIDE_EACH, NX, stride=2 * WIDE_EACH)
                source[part, member * WIDE_EACH + row] = spectrum_ref[rows, :]

    def prepare(y, carry):
        classes = cells_ref[pl.ds(y, NX, stride=WIDE), :]
        weight = jnp.where(classes == SOLID, 0.0, 1.0)
        kappa, (flow_x, flow_y, flow_z) = look_up(classes, kappa_ref, drift_ref)
        coefficient[0, y] = jnp.where(edge == NX - 1, 0.0, kappa - flow_x)
        coefficient[1, y] = jnp.where(edge == 0, 0.0, kappa + flow_x)
        coefficient[2, y] = kappa - flow_y
        coefficient[3, y] = kappa + flow_y
        coefficient[4, y] = jnp.where(lane == NZ - 1, 0.0, kappa - flow_z)
        coefficient[5, y] = jnp.where(lane == 0, 0.0, kappa + flow_z)
        real_first = first + 6.0 * kappa
        real_second = second + 6.0 * kappa
        over_first = weight / (real_first * real_first + turn * turn)
        over_second = weight / (real_second * real_second + turn * turn)
        a, b, c = real_first * over_first, turn * over_first, real_second * over_second
        coefficient[6, y] = a
        coefficient[7, y] = b
        coefficient[8, y] = c
        one, two = source[0, y], source[1, y]
        field[0, 0, y] = a * one + b * two
        field[0, 1, y] = c * two - b * one
        return carry

    lax.fori_loop(0, WIDE, prepare, 0, unroll=2)

    for sweep in range(SWEEPS):
        now, later = sweep % 2, (sweep + 1) % 2

        def row(y, carry):
            totals = []
            for part in range(2):
                here = field[now, part, y]
                total = source[part, y]
                total += coefficient[0, y] * pltpu.roll(here, NX - 1, 0) + coefficient[1, y] * pltpu.roll(here, 1, 0)
                total += coefficient[2, y] * field[now, part, y + 1] + coefficient[3, y] * field[now, part, y - 1]
                total += coefficient[4, y] * pltpu.roll(here, NZ - 1, 1) + coefficient[5, y] * pltpu.roll(here, 1, 1)
                totals.append(total)
            one, two = totals
            a, b, c = coefficient[6, y], coefficient[7, y], coefficient[8, y]
            field[later, 0, y] = a * one + b * two
            field[later, 1, y] = c * two - b * one
            return carry

        lax.fori_loop(sweep + 1, WIDE - 1 - sweep, row, 0, unroll=2)

    for member in range(MEMBERS):
        for row in range(EACH):
            for part in range(2):
                at = member * NX * 2 * EACH + part * EACH + row
                sent_ref[pl.ds(at, NX, stride=2 * EACH), :] = field[SWEEPS % 2, part, HALO + member * EACH + row]


def call(kernel, out_shape, in_specs, scratch=(), flops=1_000_000, moved=2_000_000):
    return pl.pallas_call(
        kernel,
        out_shape=out_shape,
        in_specs=in_specs,
        out_specs=jax.tree.map(lambda _: VMEM, out_shape),
        scratch_shapes=scratch,
        cost_estimate=pl.CostEstimate(flops=flops, bytes_accessed=moved, transcendentals=0),
        compiler_params=pltpu.CompilerParams(vmem_limit_bytes=GRANT),
    )


def shape(*dims):
    return jax.ShapeDtypeStruct(dims, F32)


def exchange(value, axes):
    return lax.all_to_all(value, axes, split_axis=0, concat_axis=0, tiled=True)


def local(iterate, forcing, start_field, classes, open_mask, diffusivity, drift):
    forward, back, shift = tables()
    iterate = iterate.reshape(LOCAL, NY, NZ)
    forcing = forcing.reshape(LOCAL, NY, NZ)
    start_field = start_field.reshape(NY, NZ)
    classes = classes.reshape(NY, NZ)
    open_mask = open_mask.reshape(NY, NZ)

    masked = iterate * open_mask.astype(F32)
    up = [(i, i + 1) for i in range(NX - 1)]
    down = [(j, i) for i, j in up]
    west = lax.ppermute(masked, SPACE, up)
    east = lax.ppermute(masked, SPACE, down)
    arrived = lax.ppermute(masked[LOCAL - 1], TM, [(i, i + 1) for i in range(GROUPS - 1)])

    cells = jnp.pad(jnp.where(open_mask == 1, classes, SOLID), ((HALO, HALO), (0, 0)), constant_values=SOLID)
    cells = lax.dynamic_slice_in_dim(cells, lax.axis_index(("yh", "zh")) * SPAN, WIDE, 0)
    cells = cells.reshape(1, 1, WIDE, NZ)
    for axis, dim, bit in (("yl", 0, 1), ("yl", 0, 2), ("x", 1, 1), ("x", 1, 2)):
        other = lax.ppermute(cells, axis, [(i, i ^ bit) for i in range(4)])
        upper = (lax.axis_index(axis) & bit) != 0
        pair = [jnp.where(upper, other, cells), jnp.where(upper, cells, other)]
        cells = jnp.concatenate(pair, axis=dim)
    cells = cells.reshape(NX * WIDE, NZ)

    part, side = call(
        local_terms,
        (shape(LOCAL, NY, NZ), shape(3, NY, NZ)),
        [VMEM] * 4 + [SMEM] * 2,
    )(masked, forcing, classes, open_mask, diffusivity, drift)
    first = (lax.axis_index(TM) == 0).astype(jnp.int32).reshape(1)
    residual, sent = call(
        finish_residual,
        (shape(LOCAL, NY, NZ), shape(QUARTERS * WIDE * LOCAL, NZ)),
        [VMEM] * 6 + [SMEM],
    )(part, side, east, west, start_field, arrived, first)

    steps = exchange(sent, TM).reshape(GROUPS, WIDE_EACH, LOCAL, NZ)
    sent = call(to_frequencies, shape(SLOTS * 2 * WIDE_EACH, NZ), [VMEM] * 2)(steps, jnp.asarray(forward))
    spectrum = exchange(sent.reshape(SLOTS, 1, 2 * WIDE_EACH * NZ), BLOCK).reshape(SLOTS * 2 * WIDE_EACH, NZ)
    mine = lax.dynamic_slice_in_dim(jnp.asarray(shift), lax.axis_index(BLOCK), 1, 0).reshape(4)
    sent = call(
        solve_slot,
        shape(SLOTS * 2 * EACH, NZ),
        [VMEM] * 2 + [SMEM] * 3,
        scratch=[
            pltpu.VMEM((2, WIDE, NX, NZ), F32),
            pltpu.VMEM((2, 2, WIDE, NX, NZ), F32),
            pltpu.VMEM((9, WIDE, NX, NZ), F32),
        ],
    )(spectrum, cells, diffusivity, drift, mine)
    solved = exchange(sent, BLOCK)
    sent = call(to_steps, shape(GROUPS, EACH, LOCAL, NZ), [VMEM] * 2)(solved, jnp.asarray(back))
    rows = exchange(sent.reshape(GROUPS * EACH * LOCAL, NZ), TM)
    corrected = call(to_grid, shape(LOCAL, NY, NZ), [VMEM])(rows)
    grid = (LOCAL, 1, NY, NZ)
    return residual.reshape(grid), corrected.reshape(grid)


def solution(mesh):
    fine = Mesh(mesh.devices.reshape(2, 2, 4, 2, 4, 4), AXES)
    big = P(TM, SPACE, None, None)
    plane = P(SPACE, None, None)

    return jax.shard_map(
        local,
        mesh=fine,
        in_specs=(big, big, plane, plane, plane, P(), P()),
        out_specs=(big, big),
        check_vma=False,
    )
```

```python
import jax
import jax.numpy as jnp
import numpy as np
from jax import lax
from jax.experimental import pallas as pl
from jax.experimental.pallas import tpu as pltpu
from jax.sharding import Mesh
from jax.sharding import PartitionSpec as P


SWEEPS = 4
ALPHA = 0.1
STEPS = 256
GROUPS = 32
LOCAL = STEPS // GROUPS
NX, NY, NZ = 16, 128, 128
QUARTERS = 4
MEMBERS = GROUPS // QUARTERS
SPAN = NY // QUARTERS
HALO = SWEEPS
WIDE = SPAN + 2 * HALO
WIDE_EACH = WIDE // MEMBERS
EACH = SPAN // MEMBERS
SLOTS = STEPS // 2
CLASSES = 8
SOLID = CLASSES

AXES = ("yh", "zh", "zl", "core", "yl", "x")
TM = ("yh", "zh", "zl", "core")
SPACE = ("yl", "x")
BLOCK = ("zl", "core", "yl", "x")

GRANT = 16 << 20
VMEM = pl.BlockSpec(memory_space=pltpu.VMEM)
SMEM = pl.BlockSpec(memory_space=pltpu.SMEM)
F32 = jnp.float32


def tables():
    n = np.arange(STEPS, dtype=np.float64)
    k = np.arange(SLOTS, dtype=np.float64)
    ramp = ALPHA ** (n / STEPS)
    angle = 2.0 * np.pi * ((n[None, :] * k[:, None]) % STEPS) / STEPS
    cosine, sine = np.cos(angle), np.sin(angle)
    alternate = np.where(np.arange(STEPS) % 2 == 0, 1.0, -1.0)
    real, imag = cosine.copy(), -sine
    imag[0] = alternate
    forward = np.concatenate([real, imag], axis=0) * ramp
    real, imag = 2.0 * cosine, -2.0 * sine
    real[0] = 1.0
    imag[0] = alternate
    back = np.concatenate([real, imag], axis=0) / (ramp * STEPS)
    root = ALPHA ** (1.0 / STEPS)
    base = 2.0 * np.pi * k / STEPS
    first = 1.0 - root * np.cos(base)
    second = first.copy()
    second[0] = 1.0 + root
    turn = root * np.sin(base)
    shift = np.stack([first, second, turn, np.zeros_like(turn)], axis=1)
    return forward.astype(np.float32), back.T.astype(np.float32).copy(), shift.astype(np.float32)


def look_up(classes, kappa_ref, drift_ref):
    kappa = jnp.full(classes.shape, kappa_ref[0], F32)
    flows = [jnp.full(classes.shape, drift_ref[axis, 0], F32) for axis in range(3)]
    for level in range(1, CLASSES):
        match = classes == level
        kappa = jnp.where(match, kappa_ref[level], kappa)
        flows = [jnp.where(match, drift_ref[axis, level], flows[axis]) for axis in range(3)]
    return kappa, [kappa * flow for flow in flows]


def local_terms(masked_ref, forcing_ref, classes_ref, mask_ref, kappa_ref, drift_ref, part_ref, side_ref):
    weight = mask_ref[...].astype(F32)
    kappa, (flow_x, flow_y, flow_z) = look_up(classes_ref[...], kappa_ref, drift_ref)
    row = lax.broadcasted_iota(jnp.int32, (NY, NZ), 0)
    lane = lax.broadcasted_iota(jnp.int32, (NY, NZ), 1)
    side_ref[0] = weight * (kappa - flow_x)
    side_ref[1] = weight * (kappa + flow_x)
    side_ref[2] = weight
    north = jnp.where(row == NY - 1, 0.0, weight * (kappa - flow_y))
    south = jnp.where(row == 0, 0.0, weight * (kappa + flow_y))
    upper = jnp.where(lane == NZ - 1, 0.0, weight * (kappa - flow_z))
    lower = jnp.where(lane == 0, 0.0, weight * (kappa + flow_z))
    middle = 1.0 + 6.0 * kappa
    for n in range(LOCAL):
        here = masked_ref[n]
        total = weight * forcing_ref[n] - middle * here
        total += north * pltpu.roll(here, NY - 1, 0) + south * pltpu.roll(here, 1, 0)
        total += upper * pltpu.roll(here, NZ - 1, 1) + lower * pltpu.roll(here, 1, 1)
        if n:
            total += masked_ref[n - 1]
        part_ref[n] = total


def finish_residual(part_ref, side_ref, east_ref, west_ref, start_ref, arrived_ref, first_ref, residual_ref, sent_ref):
    east, west, weight = side_ref[0], side_ref[1], side_ref[2]
    begins = first_ref[0]
    step_before = weight * jnp.where(begins == 1, start_ref[...], arrived_ref[...])
    for n in range(LOCAL):
        total = part_ref[n] + east * east_ref[n] + west * west_ref[n]
        if n == 0:
            total += step_before
        residual_ref[n] = total
        for quarter in range(QUARTERS):
            low = max(quarter * SPAN - HALO, 0)
            high = min((quarter + 1) * SPAN + HALO, NY)
            at = quarter * WIDE + low - (quarter * SPAN - HALO)
            sent_ref[pl.ds(at * LOCAL + n, high - low, stride=LOCAL), :] = total[low:high]
    outside = jnp.zeros((HALO * LOCAL, NZ), F32)
    sent_ref[0 : HALO * LOCAL, :] = outside
    sent_ref[(QUARTERS * WIDE - HALO) * LOCAL :, :] = outside


def to_frequencies(steps_ref, table_ref, sent_ref):
    fields = [steps_ref[:, row].reshape(STEPS, NZ) for row in range(WIDE_EACH)]
    spectrum = jnp.dot(
        table_ref[...],
        jnp.concatenate(fields, axis=1),
        precision=lax.Precision.HIGHEST,
        preferred_element_type=F32,
    )
    for row in range(WIDE_EACH):
        columns = spectrum[:, row * NZ : (row + 1) * NZ]
        for part in range(2):
            rows = columns[part * SLOTS : (part + 1) * SLOTS]
            sent_ref[pl.ds(part * WIDE_EACH + row, SLOTS, stride=2 * WIDE_EACH), :] = rows


def to_steps(slots_ref, table_ref, sent_ref):
    columns = []
    for row in range(EACH):
        parts = [slots_ref[pl.ds(part * EACH + row, SLOTS, stride=2 * EACH), :] for part in range(2)]
        columns.append(jnp.concatenate(parts, axis=0))
    steps = jnp.dot(
        table_ref[...],
        jnp.concatenate(columns, axis=1),
        precision=lax.Precision.HIGHEST,
        preferred_element_type=F32,
    )
    for row in range(EACH):
        sent_ref[:, row] = steps[:, row * NZ : (row + 1) * NZ].reshape(GROUPS, LOCAL, NZ)


def to_grid(rows_ref, out_ref):
    for n in range(LOCAL):
        out_ref[n] = rows_ref[pl.ds(n, NY, stride=LOCAL), :]


def prepare_slot(cells_ref, kappa_ref, drift_ref, shift_ref, coefficient_ref):
    edge = lax.broadcasted_iota(jnp.int32, (NX, NZ), 0)
    lane = lax.broadcasted_iota(jnp.int32, (NX, NZ), 1)
    first, second, turn = shift_ref[0], shift_ref[1], shift_ref[2]

    def prepare(y, carry):
        classes = cells_ref[pl.ds(y, NX, stride=WIDE), :]
        weight = jnp.where(classes == SOLID, 0.0, 1.0)
        kappa, (flow_x, flow_y, flow_z) = look_up(classes, kappa_ref, drift_ref)
        coefficient_ref[0, y] = jnp.where(edge == NX - 1, 0.0, kappa - flow_x)
        coefficient_ref[1, y] = jnp.where(edge == 0, 0.0, kappa + flow_x)
        coefficient_ref[2, y] = kappa - flow_y
        coefficient_ref[3, y] = kappa + flow_y
        coefficient_ref[4, y] = jnp.where(lane == NZ - 1, 0.0, kappa - flow_z)
        coefficient_ref[5, y] = jnp.where(lane == 0, 0.0, kappa + flow_z)
        real_first = first + 6.0 * kappa
        real_second = second + 6.0 * kappa
        over_first = weight / (real_first * real_first + turn * turn)
        over_second = weight / (real_second * real_second + turn * turn)
        coefficient_ref[6, y] = real_first * over_first
        coefficient_ref[7, y] = turn * over_first
        coefficient_ref[8, y] = real_second * over_second
        return carry

    lax.fori_loop(0, WIDE, prepare, 0, unroll=2)


def solve_slot(spectrum_ref, coefficient_ref, sent_ref, source, even, odd):
    def scale(y, one, two):
        a, b, c = coefficient_ref[6, y], coefficient_ref[7, y], coefficient_ref[8, y]
        return a * one + b * two, c * two - b * one

    blank = jnp.zeros((2, NX, NZ), F32)
    even[0] = blank
    even[WIDE + 1] = blank
    for member in range(MEMBERS):
        for row in range(WIDE_EACH):
            at = member * NX * 2 * WIDE_EACH + row
            y = member * WIDE_EACH + row
            one = spectrum_ref[pl.ds(at, NX, stride=2 * WIDE_EACH), :]
            two = spectrum_ref[pl.ds(at + WIDE_EACH, NX, stride=2 * WIDE_EACH), :]
            source[y, 0] = one
            source[y, 1] = two
            even[y + 1, 0], even[y + 1, 1] = scale(y, one, two)

    for sweep in range(SWEEPS):
        now, later = (even, odd) if sweep % 2 == 0 else (odd, even)
        begin = (sweep + 1) // 2 * 2
        end = WIDE - begin

        def row(y, carry):
            south, here = carry
            north = (now[y + 2, 0], now[y + 2, 1])
            totals = []
            for part in range(2):
                mid = here[part]
                total = source[y, part]
                total += coefficient_ref[0, y] * pltpu.roll(mid, NX - 1, 0)
                total += coefficient_ref[1, y] * pltpu.roll(mid, 1, 0)
                total += coefficient_ref[2, y] * north[part] + coefficient_ref[3, y] * south[part]
                total += coefficient_ref[4, y] * pltpu.roll(mid, NZ - 1, 1)
                total += coefficient_ref[5, y] * pltpu.roll(mid, 1, 1)
                totals.append(total)
            later[y + 1, 0], later[y + 1, 1] = scale(y, *totals)
            return here, north

        start = tuple((now[begin + k, 0], now[begin + k, 1]) for k in range(2))
        lax.fori_loop(begin, end, row, start, unroll=4)

    field = even if SWEEPS % 2 == 0 else odd
    for member in range(MEMBERS):
        for row in range(EACH):
            for part in range(2):
                at = member * NX * 2 * EACH + part * EACH + row
                sent_ref[pl.ds(at, NX, stride=2 * EACH), :] = field[HALO + member * EACH + row + 1, part]


def call(kernel, out_shape, in_specs, scratch=(), flops=1_000_000, moved=2_000_000):
    return pl.pallas_call(
        kernel,
        out_shape=out_shape,
        in_specs=in_specs,
        out_specs=jax.tree.map(lambda _: VMEM, out_shape),
        scratch_shapes=scratch,
        cost_estimate=pl.CostEstimate(flops=flops, bytes_accessed=moved, transcendentals=0),
        compiler_params=pltpu.CompilerParams(vmem_limit_bytes=GRANT),
    )


def shape(*dims):
    return jax.ShapeDtypeStruct(dims, F32)


def exchange(value, axes):
    return lax.all_to_all(value, axes, split_axis=0, concat_axis=0, tiled=True)


def local(iterate, forcing, start_field, classes, open_mask, diffusivity, drift):
    forward, back, shift = tables()
    iterate = iterate.reshape(LOCAL, NY, NZ)
    forcing = forcing.reshape(LOCAL, NY, NZ)
    start_field = start_field.reshape(NY, NZ)
    classes = classes.reshape(NY, NZ)
    open_mask = open_mask.reshape(NY, NZ)

    masked = iterate * open_mask.astype(F32)
    up = [(i, i + 1) for i in range(NX - 1)]
    down = [(j, i) for i, j in up]
    west = lax.ppermute(masked, SPACE, up)
    east = lax.ppermute(masked, SPACE, down)
    arrived = lax.ppermute(masked[LOCAL - 1], TM, [(i, i + 1) for i in range(GROUPS - 1)])

    cells = jnp.pad(jnp.where(open_mask == 1, classes, SOLID), ((HALO, HALO), (0, 0)), constant_values=SOLID)
    cells = lax.dynamic_slice_in_dim(cells, lax.axis_index(("yh", "zh")) * SPAN, WIDE, 0)
    cells = cells.reshape(1, 1, WIDE, NZ)
    for axis, dim, bit in (("yl", 0, 1), ("yl", 0, 2), ("x", 1, 1), ("x", 1, 2)):
        other = lax.ppermute(cells, axis, [(i, i ^ bit) for i in range(4)])
        upper = (lax.axis_index(axis) & bit) != 0
        pair = [jnp.where(upper, other, cells), jnp.where(upper, cells, other)]
        cells = jnp.concatenate(pair, axis=dim)
    cells = cells.reshape(NX * WIDE, NZ)

    part, side = call(
        local_terms,
        (shape(LOCAL, NY, NZ), shape(3, NY, NZ)),
        [VMEM] * 4 + [SMEM] * 2,
    )(masked, forcing, classes, open_mask, diffusivity, drift)
    first = (lax.axis_index(TM) == 0).astype(jnp.int32).reshape(1)
    residual, sent = call(
        finish_residual,
        (shape(LOCAL, NY, NZ), shape(QUARTERS * WIDE * LOCAL, NZ)),
        [VMEM] * 6 + [SMEM],
    )(part, side, east, west, start_field, arrived, first)

    steps = exchange(sent, TM).reshape(GROUPS, WIDE_EACH, LOCAL, NZ)
    sent = call(to_frequencies, shape(SLOTS * 2 * WIDE_EACH, NZ), [VMEM] * 2)(steps, jnp.asarray(forward))
    spectrum = exchange(sent.reshape(SLOTS, 1, 2 * WIDE_EACH * NZ), BLOCK).reshape(SLOTS * 2 * WIDE_EACH, NZ)
    mine = lax.dynamic_slice_in_dim(jnp.asarray(shift), lax.axis_index(BLOCK), 1, 0).reshape(4)
    coefficient = call(prepare_slot, shape(9, WIDE, NX, NZ), [VMEM] + [SMEM] * 3)(cells, diffusivity, drift, mine)
    sent = call(
        solve_slot,
        shape(SLOTS * 2 * EACH, NZ),
        [VMEM] * 2,
        scratch=[
            pltpu.VMEM((WIDE, 2, NX, NZ), F32),
            pltpu.VMEM((WIDE + 2, 2, NX, NZ), F32),
            pltpu.VMEM((WIDE + 2, 2, NX, NZ), F32),
        ],
    )(spectrum, coefficient)
    solved = exchange(sent, BLOCK)
    sent = call(to_steps, shape(GROUPS, EACH, LOCAL, NZ), [VMEM] * 2)(solved, jnp.asarray(back))
    rows = exchange(sent.reshape(GROUPS * EACH * LOCAL, NZ), TM)
    corrected = call(to_grid, shape(LOCAL, NY, NZ), [VMEM])(rows)
    grid = (LOCAL, 1, NY, NZ)
    return residual.reshape(grid), corrected.reshape(grid)


def solution(mesh):
    fine = Mesh(mesh.devices.reshape(2, 2, 4, 2, 4, 4), AXES)
    big = P(TM, SPACE, None, None)
    plane = P(SPACE, None, None)

    return jax.shard_map(
        local,
        mesh=fine,
        in_specs=(big, big, plane, plane, plane, P(), P()),
        out_specs=(big, big),
        check_vma=False,
    )
```

```python
import jax
import jax.numpy as jnp
import numpy as np
from jax import lax
from jax.experimental import pallas as pl
from jax.experimental.pallas import tpu as pltpu
from jax.sharding import Mesh
from jax.sharding import PartitionSpec as P


SWEEPS = 4
ALPHA = 0.1
STEPS = 256
GROUPS = 32
LOCAL = STEPS // GROUPS
NX, NY, NZ = 16, 128, 128
QUARTERS = 4
MEMBERS = GROUPS // QUARTERS
SPAN = NY // QUARTERS
HALO = SWEEPS
WIDE = SPAN + 2 * HALO
WIDE_EACH = WIDE // MEMBERS
EACH = SPAN // MEMBERS
SLOTS = STEPS // 2
CLASSES = 8
SOLID = CLASSES

AXES = ("yh", "zh", "zl", "core", "yl", "x")
TM = ("yh", "zh", "zl", "core")
SPACE = ("yl", "x")
BLOCK = ("zl", "core", "yl", "x")

GRANT = 16 << 20
VMEM = pl.BlockSpec(memory_space=pltpu.VMEM)
SMEM = pl.BlockSpec(memory_space=pltpu.SMEM)
F32 = jnp.float32


def tables():
    n = np.arange(STEPS, dtype=np.float64)
    k = np.arange(SLOTS, dtype=np.float64)
    ramp = ALPHA ** (n / STEPS)
    angle = 2.0 * np.pi * ((n[None, :] * k[:, None]) % STEPS) / STEPS
    cosine, sine = np.cos(angle), np.sin(angle)
    alternate = np.where(np.arange(STEPS) % 2 == 0, 1.0, -1.0)
    real, imag = cosine.copy(), -sine
    imag[0] = alternate
    forward = np.concatenate([real, imag], axis=0) * ramp
    real, imag = 2.0 * cosine, -2.0 * sine
    real[0] = 1.0
    imag[0] = alternate
    back = np.concatenate([real, imag], axis=0) / (ramp * STEPS)
    root = ALPHA ** (1.0 / STEPS)
    base = 2.0 * np.pi * k / STEPS
    first = 1.0 - root * np.cos(base)
    second = first.copy()
    second[0] = 1.0 + root
    turn = root * np.sin(base)
    shift = np.stack([first, second, turn, np.zeros_like(turn)], axis=1)
    return forward.astype(np.float32), back.T.astype(np.float32).copy(), shift.astype(np.float32)


def look_up(classes, class_ref):
    found = [jnp.full(classes.shape, class_ref[kind, 0], F32) for kind in range(4)]
    for level in range(1, CLASSES):
        match = classes == level
        found = [jnp.where(match, class_ref[kind, level], found[kind]) for kind in range(4)]
    kappa, *tilts = found
    return jnp.where(classes == SOLID, 0.0, 1.0), kappa, [kappa * tilt for tilt in tilts]


def local_terms(masked_ref, forcing_ref, cells_ref, class_ref, part_ref, side_ref):
    weight, kappa, (flow_x, flow_y, flow_z) = look_up(cells_ref[...], class_ref)
    row = lax.broadcasted_iota(jnp.int32, (NY, NZ), 0)
    lane = lax.broadcasted_iota(jnp.int32, (NY, NZ), 1)
    side_ref[0] = weight * (kappa - flow_x)
    side_ref[1] = weight * (kappa + flow_x)
    side_ref[2] = weight
    north = jnp.where(row == NY - 1, 0.0, weight * (kappa - flow_y))
    south = jnp.where(row == 0, 0.0, weight * (kappa + flow_y))
    upper = jnp.where(lane == NZ - 1, 0.0, weight * (kappa - flow_z))
    lower = jnp.where(lane == 0, 0.0, weight * (kappa + flow_z))
    middle = 1.0 + 6.0 * kappa
    for n in range(LOCAL):
        here = masked_ref[n]
        total = weight * forcing_ref[n] - middle * here
        total += north * pltpu.roll(here, NY - 1, 0) + south * pltpu.roll(here, 1, 0)
        total += upper * pltpu.roll(here, NZ - 1, 1) + lower * pltpu.roll(here, 1, 1)
        if n:
            total += masked_ref[n - 1]
        part_ref[n] = total


def finish_residual(part_ref, side_ref, east_ref, west_ref, start_ref, arrived_ref, first_ref, residual_ref, sent_ref):
    east, west, weight = side_ref[0], side_ref[1], side_ref[2]
    begins = first_ref[0]
    step_before = weight * jnp.where(begins == 1, start_ref[...], arrived_ref[...])
    for n in range(LOCAL):
        total = part_ref[n] + east * east_ref[n] + west * west_ref[n]
        if n == 0:
            total += step_before
        residual_ref[n] = total
        for quarter in range(QUARTERS):
            low = max(quarter * SPAN - HALO, 0)
            high = min((quarter + 1) * SPAN + HALO, NY)
            at = quarter * WIDE + low - (quarter * SPAN - HALO)
            sent_ref[pl.ds(at * LOCAL + n, high - low, stride=LOCAL), :] = total[low:high]
    outside = jnp.zeros((HALO * LOCAL, NZ), F32)
    sent_ref[0 : HALO * LOCAL, :] = outside
    sent_ref[(QUARTERS * WIDE - HALO) * LOCAL :, :] = outside


def to_frequencies(steps_ref, table_ref, sent_ref):
    fields = [steps_ref[:, row].reshape(STEPS, NZ) for row in range(WIDE_EACH)]
    spectrum = jnp.dot(
        table_ref[...],
        jnp.concatenate(fields, axis=1),
        precision=lax.Precision.HIGHEST,
        preferred_element_type=F32,
    )
    for row in range(WIDE_EACH):
        columns = spectrum[:, row * NZ : (row + 1) * NZ]
        for part in range(2):
            rows = columns[part * SLOTS : (part + 1) * SLOTS]
            sent_ref[pl.ds(part * WIDE_EACH + row, SLOTS, stride=2 * WIDE_EACH), :] = rows


def to_steps(slots_ref, table_ref, sent_ref):
    columns = []
    for row in range(EACH):
        parts = [slots_ref[pl.ds(part * EACH + row, SLOTS, stride=2 * EACH), :] for part in range(2)]
        columns.append(jnp.concatenate(parts, axis=0))
    steps = jnp.dot(
        table_ref[...],
        jnp.concatenate(columns, axis=1),
        precision=lax.Precision.HIGHEST,
        preferred_element_type=F32,
    )
    for row in range(EACH):
        sent_ref[:, row] = steps[:, row * NZ : (row + 1) * NZ].reshape(GROUPS, LOCAL, NZ)


def to_grid(rows_ref, out_ref):
    for n in range(LOCAL):
        out_ref[n] = rows_ref[pl.ds(n, NY, stride=LOCAL), :]


def prepare_slot(cells_ref, class_ref, shift_ref, coefficient_ref):
    edge = lax.broadcasted_iota(jnp.int32, (NX, NZ), 0)
    lane = lax.broadcasted_iota(jnp.int32, (NX, NZ), 1)
    first, second, turn = shift_ref[0], shift_ref[1], shift_ref[2]

    def prepare(y, carry):
        weight, kappa, (flow_x, flow_y, flow_z) = look_up(cells_ref[pl.ds(y, NX, stride=WIDE), :], class_ref)
        coefficient_ref[0, y] = jnp.where(edge == NX - 1, 0.0, kappa - flow_x)
        coefficient_ref[1, y] = jnp.where(edge == 0, 0.0, kappa + flow_x)
        coefficient_ref[2, y] = kappa - flow_y
        coefficient_ref[3, y] = kappa + flow_y
        coefficient_ref[4, y] = jnp.where(lane == NZ - 1, 0.0, kappa - flow_z)
        coefficient_ref[5, y] = jnp.where(lane == 0, 0.0, kappa + flow_z)
        real_first = first + 6.0 * kappa
        real_second = second + 6.0 * kappa
        over_first = weight / (real_first * real_first + turn * turn)
        over_second = weight / (real_second * real_second + turn * turn)
        coefficient_ref[6, y] = real_first * over_first
        coefficient_ref[7, y] = turn * over_first
        coefficient_ref[8, y] = real_second * over_second
        return carry

    lax.fori_loop(0, WIDE, prepare, 0, unroll=2)


def solve_slot(spectrum_ref, coefficient_ref, sent_ref, source, even, odd):
    def scale(y, one, two):
        a, b, c = coefficient_ref[6, y], coefficient_ref[7, y], coefficient_ref[8, y]
        return a * one + b * two, c * two - b * one

    blank = jnp.zeros((2, NX, NZ), F32)
    even[0] = blank
    even[WIDE + 1] = blank
    for member in range(MEMBERS):
        for row in range(WIDE_EACH):
            at = member * NX * 2 * WIDE_EACH + row
            y = member * WIDE_EACH + row
            one = spectrum_ref[pl.ds(at, NX, stride=2 * WIDE_EACH), :]
            two = spectrum_ref[pl.ds(at + WIDE_EACH, NX, stride=2 * WIDE_EACH), :]
            source[y, 0] = one
            source[y, 1] = two
            even[y + 1, 0], even[y + 1, 1] = scale(y, one, two)

    for sweep in range(SWEEPS):
        now, later = (even, odd) if sweep % 2 == 0 else (odd, even)
        begin = (sweep + 1) // 2 * 2
        end = WIDE - begin

        def row(y, carry):
            south, here = carry
            north = (now[y + 2, 0], now[y + 2, 1])
            totals = []
            for part in range(2):
                mid = here[part]
                total = source[y, part]
                total += coefficient_ref[0, y] * pltpu.roll(mid, NX - 1, 0)
                total += coefficient_ref[1, y] * pltpu.roll(mid, 1, 0)
                total += coefficient_ref[2, y] * north[part] + coefficient_ref[3, y] * south[part]
                total += coefficient_ref[4, y] * pltpu.roll(mid, NZ - 1, 1)
                total += coefficient_ref[5, y] * pltpu.roll(mid, 1, 1)
                totals.append(total)
            later[y + 1, 0], later[y + 1, 1] = scale(y, *totals)
            return here, north

        start = tuple((now[begin + k, 0], now[begin + k, 1]) for k in range(2))
        lax.fori_loop(begin, end, row, start, unroll=4)

    field = even if SWEEPS % 2 == 0 else odd
    for member in range(MEMBERS):
        for row in range(EACH):
            for part in range(2):
                at = member * NX * 2 * EACH + part * EACH + row
                sent_ref[pl.ds(at, NX, stride=2 * EACH), :] = field[HALO + member * EACH + row + 1, part]


def call(kernel, out_shape, in_specs, scratch=(), flops=1_000_000, moved=2_000_000):
    return pl.pallas_call(
        kernel,
        out_shape=out_shape,
        in_specs=in_specs,
        out_specs=jax.tree.map(lambda _: VMEM, out_shape),
        scratch_shapes=scratch,
        cost_estimate=pl.CostEstimate(flops=flops, bytes_accessed=moved, transcendentals=0),
        compiler_params=pltpu.CompilerParams(vmem_limit_bytes=GRANT),
    )


def shape(*dims):
    return jax.ShapeDtypeStruct(dims, F32)


def exchange(value, axes):
    return lax.all_to_all(value, axes, split_axis=0, concat_axis=0, tiled=True)


def local(iterate, forcing, start_field, classes, open_mask, diffusivity, drift):
    forward, back, shift = tables()
    iterate = iterate.reshape(LOCAL, NY, NZ)
    forcing = forcing.reshape(LOCAL, NY, NZ)
    start_field = start_field.reshape(NY, NZ)
    classes = classes.reshape(NY, NZ)
    open_mask = open_mask.reshape(NY, NZ)

    cells = lax.optimization_barrier(jnp.where(open_mask == 1, classes, SOLID))
    masked = iterate * (cells != SOLID).astype(F32)
    per_class = jnp.concatenate([diffusivity[None], drift])
    up = [(i, i + 1) for i in range(NX - 1)]
    down = [(j, i) for i, j in up]
    west = lax.ppermute(masked, SPACE, up)
    east = lax.ppermute(masked, SPACE, down)
    arrived = lax.ppermute(masked[LOCAL - 1], TM, [(i, i + 1) for i in range(GROUPS - 1)])

    plane = cells
    cells = jnp.pad(cells, ((HALO, HALO), (0, 0)), constant_values=SOLID)
    cells = lax.dynamic_slice_in_dim(cells, lax.axis_index(("yh", "zh")) * SPAN, WIDE, 0)
    cells = cells.reshape(1, 1, WIDE, NZ)
    for axis, dim, bit in (("yl", 0, 1), ("yl", 0, 2), ("x", 1, 1), ("x", 1, 2)):
        other = lax.ppermute(cells, axis, [(i, i ^ bit) for i in range(4)])
        upper = (lax.axis_index(axis) & bit) != 0
        pair = [jnp.where(upper, other, cells), jnp.where(upper, cells, other)]
        cells = jnp.concatenate(pair, axis=dim)
    cells = cells.reshape(NX * WIDE, NZ)

    part, side = call(
        local_terms,
        (shape(LOCAL, NY, NZ), shape(3, NY, NZ)),
        [VMEM] * 3 + [SMEM],
    )(masked, forcing, plane, per_class)
    first = (lax.axis_index(TM) == 0).astype(jnp.int32).reshape(1)
    residual, sent = call(
        finish_residual,
        (shape(LOCAL, NY, NZ), shape(QUARTERS * WIDE * LOCAL, NZ)),
        [VMEM] * 6 + [SMEM],
    )(part, side, east, west, start_field, arrived, first)

    steps = exchange(sent, TM).reshape(GROUPS, WIDE_EACH, LOCAL, NZ)
    sent = call(to_frequencies, shape(SLOTS * 2 * WIDE_EACH, NZ), [VMEM] * 2)(steps, jnp.asarray(forward))
    spectrum = exchange(sent.reshape(SLOTS, 1, 2 * WIDE_EACH * NZ), BLOCK).reshape(SLOTS * 2 * WIDE_EACH, NZ)
    mine = lax.dynamic_slice_in_dim(jnp.asarray(shift), lax.axis_index(BLOCK), 1, 0).reshape(4)
    coefficient = call(prepare_slot, shape(9, WIDE, NX, NZ), [VMEM] + [SMEM] * 2)(cells, per_class, mine)
    sent = call(
        solve_slot,
        shape(SLOTS * 2 * EACH, NZ),
        [VMEM] * 2,
        scratch=[
            pltpu.VMEM((WIDE, 2, NX, NZ), F32),
            pltpu.VMEM((WIDE + 2, 2, NX, NZ), F32),
            pltpu.VMEM((WIDE + 2, 2, NX, NZ), F32),
        ],
    )(spectrum, coefficient)
    solved = exchange(sent, BLOCK)
    sent = call(to_steps, shape(GROUPS, EACH, LOCAL, NZ), [VMEM] * 2)(solved, jnp.asarray(back))
    rows = exchange(sent.reshape(GROUPS * EACH * LOCAL, NZ), TM)
    corrected = call(to_grid, shape(LOCAL, NY, NZ), [VMEM])(rows)
    grid = (LOCAL, 1, NY, NZ)
    return residual.reshape(grid), corrected.reshape(grid)


def solution(mesh):
    fine = Mesh(mesh.devices.reshape(2, 2, 4, 2, 4, 4), AXES)
    big = P(TM, SPACE, None, None)
    plane = P(SPACE, None, None)

    return jax.shard_map(
        local,
        mesh=fine,
        in_specs=(big, big, plane, plane, plane, P(), P()),
        out_specs=(big, big),
        check_vma=False,
    )
```

```python
import jax
import jax.numpy as jnp
import numpy as np
from jax import lax
from jax.experimental import pallas as pl
from jax.experimental.pallas import tpu as pltpu
from jax.sharding import Mesh
from jax.sharding import PartitionSpec as P


SWEEPS = 4
ALPHA = 0.1
STEPS = 256
GROUPS = 32
LOCAL = STEPS // GROUPS
NX, NY, NZ = 16, 128, 128
QUARTERS = 4
MEMBERS = GROUPS // QUARTERS
SPAN = NY // QUARTERS
HALO = SWEEPS
WIDE = SPAN + 2 * HALO
WIDE_EACH = WIDE // MEMBERS
EACH = SPAN // MEMBERS
SLOTS = STEPS // 2
CLASSES = 8
SOLID = CLASSES

AXES = ("yh", "zh", "zl", "core", "yl", "x")
TM = ("yh", "zh", "zl", "core")
SPACE = ("yl", "x")
BLOCK = ("zl", "core", "yl", "x")

GRANT = 16 << 20
VMEM = pl.BlockSpec(memory_space=pltpu.VMEM)
SMEM = pl.BlockSpec(memory_space=pltpu.SMEM)
F32 = jnp.float32


def tables():
    n = np.arange(STEPS, dtype=np.float64)
    k = np.arange(SLOTS, dtype=np.float64)
    ramp = ALPHA ** (n / STEPS)
    angle = 2.0 * np.pi * ((n[None, :] * k[:, None]) % STEPS) / STEPS
    cosine, sine = np.cos(angle), np.sin(angle)
    alternate = np.where(np.arange(STEPS) % 2 == 0, 1.0, -1.0)
    real, imag = cosine.copy(), -sine
    imag[0] = alternate
    forward = np.concatenate([real, imag], axis=0) * ramp
    real, imag = 2.0 * cosine, -2.0 * sine
    real[0] = 1.0
    imag[0] = alternate
    back = np.concatenate([real, imag], axis=0) / (ramp * STEPS)
    root = ALPHA ** (1.0 / STEPS)
    base = 2.0 * np.pi * k / STEPS
    first = 1.0 - root * np.cos(base)
    second = first.copy()
    second[0] = 1.0 + root
    turn = root * np.sin(base)
    shift = np.stack([first, second, turn, np.zeros_like(turn)], axis=1)
    return forward.astype(np.float32), back.T.astype(np.float32).copy(), shift.astype(np.float32)


def look_up(classes, class_ref):
    found = [jnp.full(classes.shape, class_ref[kind, 0], F32) for kind in range(4)]
    for level in range(1, CLASSES):
        match = classes == level
        found = [jnp.where(match, class_ref[kind, level], found[kind]) for kind in range(4)]
    kappa, *tilts = found
    return jnp.where(classes == SOLID, 0.0, 1.0), kappa, [kappa * tilt for tilt in tilts]


def local_terms(masked_ref, forcing_ref, cells_ref, start_ref, class_ref, first_ref, part_ref, side_ref):
    weight, kappa, (flow_x, flow_y, flow_z) = look_up(cells_ref[...], class_ref)
    row = lax.broadcasted_iota(jnp.int32, (NY, NZ), 0)
    lane = lax.broadcasted_iota(jnp.int32, (NY, NZ), 1)
    side_ref[0] = weight * (kappa - flow_x)
    side_ref[1] = weight * (kappa + flow_x)
    side_ref[2] = weight
    north = jnp.where(row == NY - 1, 0.0, weight * (kappa - flow_y))
    south = jnp.where(row == 0, 0.0, weight * (kappa + flow_y))
    upper = jnp.where(lane == NZ - 1, 0.0, weight * (kappa - flow_z))
    lower = jnp.where(lane == 0, 0.0, weight * (kappa + flow_z))
    middle = 1.0 + 6.0 * kappa
    for n in range(LOCAL):
        here = masked_ref[n]
        total = weight * forcing_ref[n] - middle * here
        total += north * pltpu.roll(here, NY - 1, 0) + south * pltpu.roll(here, 1, 0)
        total += upper * pltpu.roll(here, NZ - 1, 1) + lower * pltpu.roll(here, 1, 1)
        total += masked_ref[n - 1] if n else weight * jnp.where(first_ref[0] == 1, start_ref[...], 0.0)
        part_ref[n] = total


def finish_residual(part_ref, side_ref, east_ref, west_ref, arrived_ref, residual_ref, sent_ref):
    east, west, weight = side_ref[0], side_ref[1], side_ref[2]
    for n in range(LOCAL):
        total = part_ref[n] + east * east_ref[n] + west * west_ref[n]
        if n == 0:
            total += weight * arrived_ref[...]
        residual_ref[n] = total
        for quarter in range(QUARTERS):
            low = max(quarter * SPAN - HALO, 0)
            high = min((quarter + 1) * SPAN + HALO, NY)
            at = quarter * WIDE + low - (quarter * SPAN - HALO)
            sent_ref[pl.ds(at * LOCAL + n, high - low, stride=LOCAL), :] = total[low:high]
    outside = jnp.zeros((HALO * LOCAL, NZ), F32)
    sent_ref[0 : HALO * LOCAL, :] = outside
    sent_ref[(QUARTERS * WIDE - HALO) * LOCAL :, :] = outside


def to_frequencies(steps_ref, table_ref, sent_ref):
    fields = [steps_ref[:, row].reshape(STEPS, NZ) for row in range(WIDE_EACH)]
    spectrum = jnp.dot(
        table_ref[...],
        jnp.concatenate(fields, axis=1),
        precision=lax.Precision.HIGHEST,
        preferred_element_type=F32,
    )
    for row in range(WIDE_EACH):
        columns = spectrum[:, row * NZ : (row + 1) * NZ]
        for part in range(2):
            rows = columns[part * SLOTS : (part + 1) * SLOTS]
            sent_ref[pl.ds(part * WIDE_EACH + row, SLOTS, stride=2 * WIDE_EACH), :] = rows


def to_steps(slots_ref, table_ref, sent_ref):
    columns = []
    for row in range(EACH):
        parts = [slots_ref[pl.ds(part * EACH + row, SLOTS, stride=2 * EACH), :] for part in range(2)]
        columns.append(jnp.concatenate(parts, axis=0))
    steps = jnp.dot(
        table_ref[...],
        jnp.concatenate(columns, axis=1),
        precision=lax.Precision.HIGHEST,
        preferred_element_type=F32,
    )
    for row in range(EACH):
        sent_ref[:, row] = steps[:, row * NZ : (row + 1) * NZ].reshape(GROUPS, LOCAL, NZ)


def to_grid(rows_ref, out_ref):
    for n in range(LOCAL):
        out_ref[n] = rows_ref[pl.ds(n, NY, stride=LOCAL), :]


def prepare_slot(cells_ref, class_ref, shift_ref, coefficient_ref):
    edge = lax.broadcasted_iota(jnp.int32, (NX, NZ), 0)
    lane = lax.broadcasted_iota(jnp.int32, (NX, NZ), 1)
    first, second, turn = shift_ref[0], shift_ref[1], shift_ref[2]

    def prepare(y, carry):
        weight, kappa, (flow_x, flow_y, flow_z) = look_up(cells_ref[pl.ds(y, NX, stride=WIDE), :], class_ref)
        coefficient_ref[0, y] = jnp.where(edge == NX - 1, 0.0, kappa - flow_x)
        coefficient_ref[1, y] = jnp.where(edge == 0, 0.0, kappa + flow_x)
        coefficient_ref[2, y] = kappa - flow_y
        coefficient_ref[3, y] = kappa + flow_y
        coefficient_ref[4, y] = jnp.where(lane == NZ - 1, 0.0, kappa - flow_z)
        coefficient_ref[5, y] = jnp.where(lane == 0, 0.0, kappa + flow_z)
        real_first = first + 6.0 * kappa
        real_second = second + 6.0 * kappa
        over_first = weight / (real_first * real_first + turn * turn)
        over_second = weight / (real_second * real_second + turn * turn)
        coefficient_ref[6, y] = real_first * over_first
        coefficient_ref[7, y] = turn * over_first
        coefficient_ref[8, y] = real_second * over_second
        return carry

    lax.fori_loop(0, WIDE, prepare, 0, unroll=2)


def solve_slot(spectrum_ref, coefficient_ref, sent_ref, source, even, odd):
    def scale(y, one, two):
        a, b, c = coefficient_ref[6, y], coefficient_ref[7, y], coefficient_ref[8, y]
        return a * one + b * two, c * two - b * one

    blank = jnp.zeros((2, NX, NZ), F32)
    even[0] = blank
    even[WIDE + 1] = blank
    for member in range(MEMBERS):
        for row in range(WIDE_EACH):
            at = member * NX * 2 * WIDE_EACH + row
            y = member * WIDE_EACH + row
            one = spectrum_ref[pl.ds(at, NX, stride=2 * WIDE_EACH), :]
            two = spectrum_ref[pl.ds(at + WIDE_EACH, NX, stride=2 * WIDE_EACH), :]
            source[y, 0] = one
            source[y, 1] = two
            even[y + 1, 0], even[y + 1, 1] = scale(y, one, two)

    for sweep in range(SWEEPS):
        now, later = (even, odd) if sweep % 2 == 0 else (odd, even)
        begin = (sweep + 1) // 2 * 2
        end = WIDE - begin

        def row(y, carry):
            south, here = carry
            north = (now[y + 2, 0], now[y + 2, 1])
            totals = []
            for part in range(2):
                mid = here[part]
                total = source[y, part]
                total += coefficient_ref[0, y] * pltpu.roll(mid, NX - 1, 0)
                total += coefficient_ref[1, y] * pltpu.roll(mid, 1, 0)
                total += coefficient_ref[2, y] * north[part] + coefficient_ref[3, y] * south[part]
                total += coefficient_ref[4, y] * pltpu.roll(mid, NZ - 1, 1)
                total += coefficient_ref[5, y] * pltpu.roll(mid, 1, 1)
                totals.append(total)
            later[y + 1, 0], later[y + 1, 1] = scale(y, *totals)
            return here, north

        start = tuple((now[begin + k, 0], now[begin + k, 1]) for k in range(2))
        lax.fori_loop(begin, end, row, start, unroll=4)

    field = even if SWEEPS % 2 == 0 else odd
    for member in range(MEMBERS):
        for row in range(EACH):
            for part in range(2):
                at = member * NX * 2 * EACH + part * EACH + row
                sent_ref[pl.ds(at, NX, stride=2 * EACH), :] = field[HALO + member * EACH + row + 1, part]


def call(kernel, out_shape, in_specs, scratch=(), flops=1_000_000, moved=2_000_000):
    return pl.pallas_call(
        kernel,
        out_shape=out_shape,
        in_specs=in_specs,
        out_specs=jax.tree.map(lambda _: VMEM, out_shape),
        scratch_shapes=scratch,
        cost_estimate=pl.CostEstimate(flops=flops, bytes_accessed=moved, transcendentals=0),
        compiler_params=pltpu.CompilerParams(vmem_limit_bytes=GRANT),
    )


def shape(*dims):
    return jax.ShapeDtypeStruct(dims, F32)


def exchange(value, axes):
    return lax.all_to_all(value, axes, split_axis=0, concat_axis=0, tiled=True)


def local(iterate, forcing, start_field, classes, open_mask, diffusivity, drift):
    forward, back, shift = tables()
    iterate = iterate.reshape(LOCAL, NY, NZ)
    forcing = forcing.reshape(LOCAL, NY, NZ)
    start_field = start_field.reshape(NY, NZ)
    classes = classes.reshape(NY, NZ)
    open_mask = open_mask.reshape(NY, NZ)

    cells = lax.optimization_barrier(jnp.where(open_mask == 1, classes, SOLID))
    masked = iterate * (cells != SOLID).astype(F32)
    per_class = jnp.concatenate([diffusivity[None], drift])
    up = [(i, i + 1) for i in range(NX - 1)]
    down = [(j, i) for i, j in up]
    west = lax.ppermute(masked, SPACE, up)
    east = lax.ppermute(masked, SPACE, down)
    arrived = lax.ppermute(masked[LOCAL - 1], TM, [(i, i + 1) for i in range(GROUPS - 1)])

    plane = cells
    cells = jnp.pad(cells, ((HALO, HALO), (0, 0)), constant_values=SOLID)
    cells = lax.dynamic_slice_in_dim(cells, lax.axis_index(("yh", "zh")) * SPAN, WIDE, 0)
    cells = cells.reshape(1, 1, WIDE, NZ)
    for axis, dim, bit in (("yl", 0, 1), ("yl", 0, 2), ("x", 1, 1), ("x", 1, 2)):
        other = lax.ppermute(cells, axis, [(i, i ^ bit) for i in range(4)])
        upper = (lax.axis_index(axis) & bit) != 0
        pair = [jnp.where(upper, other, cells), jnp.where(upper, cells, other)]
        cells = jnp.concatenate(pair, axis=dim)
    cells = cells.reshape(NX * WIDE, NZ)

    first = (lax.axis_index(TM) == 0).astype(jnp.int32).reshape(1)
    part, side = call(
        local_terms,
        (shape(LOCAL, NY, NZ), shape(3, NY, NZ)),
        [VMEM] * 4 + [SMEM] * 2,
    )(masked, forcing, plane, start_field, per_class, first)
    residual, sent = call(
        finish_residual,
        (shape(LOCAL, NY, NZ), shape(QUARTERS * WIDE * LOCAL, NZ)),
        [VMEM] * 5,
    )(part, side, east, west, arrived)

    steps = exchange(sent, TM).reshape(GROUPS, WIDE_EACH, LOCAL, NZ)
    sent = call(to_frequencies, shape(SLOTS * 2 * WIDE_EACH, NZ), [VMEM] * 2)(steps, jnp.asarray(forward))
    spectrum = exchange(sent.reshape(SLOTS, 1, 2 * WIDE_EACH * NZ), BLOCK).reshape(SLOTS * 2 * WIDE_EACH, NZ)
    mine = lax.dynamic_slice_in_dim(jnp.asarray(shift), lax.axis_index(BLOCK), 1, 0).reshape(4)
    coefficient = call(prepare_slot, shape(9, WIDE, NX, NZ), [VMEM] + [SMEM] * 2)(cells, per_class, mine)
    sent = call(
        solve_slot,
        shape(SLOTS * 2 * EACH, NZ),
        [VMEM] * 2,
        scratch=[
            pltpu.VMEM((WIDE, 2, NX, NZ), F32),
            pltpu.VMEM((WIDE + 2, 2, NX, NZ), F32),
            pltpu.VMEM((WIDE + 2, 2, NX, NZ), F32),
        ],
    )(spectrum, coefficient)
    solved = exchange(sent, BLOCK)
    sent = call(to_steps, shape(GROUPS, EACH, LOCAL, NZ), [VMEM] * 2)(solved, jnp.asarray(back))
    rows = exchange(sent.reshape(GROUPS * EACH * LOCAL, NZ), TM)
    corrected = call(to_grid, shape(LOCAL, NY, NZ), [VMEM])(rows)
    grid = (LOCAL, 1, NY, NZ)
    return residual.reshape(grid), corrected.reshape(grid)


def solution(mesh):
    fine = Mesh(mesh.devices.reshape(2, 2, 4, 2, 4, 4), AXES)
    big = P(TM, SPACE, None, None)
    plane = P(SPACE, None, None)

    return jax.shard_map(
        local,
        mesh=fine,
        in_specs=(big, big, plane, plane, plane, P(), P()),
        out_specs=(big, big),
        check_vma=False,
    )
```

```python
import jax
import jax.numpy as jnp
import numpy as np
from jax import lax
from jax.experimental import pallas as pl
from jax.experimental.pallas import tpu as pltpu
from jax.sharding import Mesh
from jax.sharding import PartitionSpec as P


SWEEPS = 4
ALPHA = 0.1
STEPS = 256
GROUPS = 32
LOCAL = STEPS // GROUPS
NX, NY, NZ = 16, 128, 128
QUARTERS = 4
MEMBERS = GROUPS // QUARTERS
SPAN = NY // QUARTERS
HALO = SWEEPS
WIDE = SPAN + 2 * HALO
WIDE_EACH = WIDE // MEMBERS
EACH = SPAN // MEMBERS
SLOTS = STEPS // 2
CLASSES = 8
SOLID = CLASSES

AXES = ("yh", "zh", "zl", "core", "yl", "x")
TM = ("yh", "zh", "zl", "core")
SPACE = ("yl", "x")
BLOCK = ("zl", "core", "yl", "x")

GRANT = 16 << 20
VMEM = pl.BlockSpec(memory_space=pltpu.VMEM)
SMEM = pl.BlockSpec(memory_space=pltpu.SMEM)
F32 = jnp.float32


def tables():
    n = np.arange(STEPS, dtype=np.float64)
    k = np.arange(SLOTS, dtype=np.float64)
    ramp = ALPHA ** (n / STEPS)
    angle = 2.0 * np.pi * ((n[None, :] * k[:, None]) % STEPS) / STEPS
    cosine, sine = np.cos(angle), np.sin(angle)
    alternate = np.where(np.arange(STEPS) % 2 == 0, 1.0, -1.0)
    real, imag = cosine.copy(), -sine
    imag[0] = alternate
    forward = np.concatenate([real, imag], axis=0) * ramp
    real, imag = 2.0 * cosine, -2.0 * sine
    real[0] = 1.0
    imag[0] = alternate
    back = np.concatenate([real, imag], axis=0) / (ramp * STEPS)
    root = ALPHA ** (1.0 / STEPS)
    base = 2.0 * np.pi * k / STEPS
    first = 1.0 - root * np.cos(base)
    second = first.copy()
    second[0] = 1.0 + root
    turn = root * np.sin(base)
    shift = np.stack([first, second, turn, np.zeros_like(turn)], axis=1)
    return forward.astype(np.float32), back.T.astype(np.float32).copy(), shift.astype(np.float32)


def look_up(classes, class_ref):
    found = [jnp.full(classes.shape, class_ref[kind, 0], F32) for kind in range(4)]
    for level in range(1, CLASSES):
        match = classes == level
        found = [jnp.where(match, class_ref[kind, level], found[kind]) for kind in range(4)]
    kappa, *tilts = found
    return jnp.where(classes == SOLID, 0.0, 1.0), kappa, [kappa * tilt for tilt in tilts]


def local_terms(masked_ref, forcing_ref, cells_ref, start_ref, class_ref, first_ref, part_ref, side_ref):
    weight, kappa, (flow_x, flow_y, flow_z) = look_up(cells_ref[...], class_ref)
    row = lax.broadcasted_iota(jnp.int32, (NY, NZ), 0)
    lane = lax.broadcasted_iota(jnp.int32, (NY, NZ), 1)
    side_ref[0] = weight * (kappa - flow_x)
    side_ref[1] = weight * (kappa + flow_x)
    side_ref[2] = weight
    north = jnp.where(row == NY - 1, 0.0, weight * (kappa - flow_y))
    south = jnp.where(row == 0, 0.0, weight * (kappa + flow_y))
    upper = jnp.where(lane == NZ - 1, 0.0, weight * (kappa - flow_z))
    lower = jnp.where(lane == 0, 0.0, weight * (kappa + flow_z))
    middle = 1.0 + 6.0 * kappa
    for n in range(LOCAL):
        here = masked_ref[n]
        total = weight * forcing_ref[n] - middle * here
        total += north * pltpu.roll(here, NY - 1, 0) + south * pltpu.roll(here, 1, 0)
        total += upper * pltpu.roll(here, NZ - 1, 1) + lower * pltpu.roll(here, 1, 1)
        total += masked_ref[n - 1] if n else weight * jnp.where(first_ref[0] == 1, start_ref[...], 0.0)
        part_ref[n] = total


def finish_residual(part_ref, side_ref, east_ref, west_ref, arrived_ref, residual_ref, sent_ref):
    east, west, weight = side_ref[0], side_ref[1], side_ref[2]
    for n in range(LOCAL):
        total = part_ref[n] + east * east_ref[n] + west * west_ref[n]
        if n == 0:
            total += weight * arrived_ref[...]
        residual_ref[n] = total
        for quarter in range(QUARTERS):
            low = max(quarter * SPAN - HALO, 0)
            high = min((quarter + 1) * SPAN + HALO, NY)
            at = quarter * WIDE + low - (quarter * SPAN - HALO)
            sent_ref[pl.ds(at * LOCAL + n, high - low, stride=LOCAL), :] = total[low:high]
    outside = jnp.zeros((HALO * LOCAL, NZ), F32)
    sent_ref[0 : HALO * LOCAL, :] = outside
    sent_ref[(QUARTERS * WIDE - HALO) * LOCAL :, :] = outside


def to_frequencies(steps_ref, table_ref, sent_ref):
    fields = [steps_ref[:, row].reshape(STEPS, NZ) for row in range(WIDE_EACH)]
    spectrum = jnp.dot(
        table_ref[...],
        jnp.concatenate(fields, axis=1),
        precision=lax.Precision.HIGHEST,
        preferred_element_type=F32,
    )
    for row in range(WIDE_EACH):
        columns = spectrum[:, row * NZ : (row + 1) * NZ]
        for part in range(2):
            rows = columns[part * SLOTS : (part + 1) * SLOTS]
            sent_ref[pl.ds(part * WIDE_EACH + row, SLOTS, stride=2 * WIDE_EACH), :] = rows


def to_steps(slots_ref, table_ref, sent_ref):
    columns = []
    for row in range(EACH):
        parts = [slots_ref[pl.ds(part * EACH + row, SLOTS, stride=2 * EACH), :] for part in range(2)]
        columns.append(jnp.concatenate(parts, axis=0))
    steps = jnp.dot(
        table_ref[...],
        jnp.concatenate(columns, axis=1),
        precision=lax.Precision.HIGHEST,
        preferred_element_type=F32,
    )
    for row in range(EACH):
        sent_ref[:, row] = steps[:, row * NZ : (row + 1) * NZ].reshape(GROUPS, LOCAL, NZ)


def to_grid(rows_ref, out_ref):
    for n in range(LOCAL):
        out_ref[n] = rows_ref[pl.ds(n, NY, stride=LOCAL), :]


def prepare_slot(cells_ref, class_ref, shift_ref, coefficient_ref):
    edge = lax.broadcasted_iota(jnp.int32, (NX, NZ), 0)
    lane = lax.broadcasted_iota(jnp.int32, (NX, NZ), 1)
    first, second, turn = shift_ref[0], shift_ref[1], shift_ref[2]

    def prepare(y, carry):
        weight, kappa, (flow_x, flow_y, flow_z) = look_up(cells_ref[pl.ds(y, NX, stride=WIDE), :], class_ref)
        coefficient_ref[0, y] = jnp.where(edge == NX - 1, 0.0, kappa - flow_x)
        coefficient_ref[1, y] = jnp.where(edge == 0, 0.0, kappa + flow_x)
        coefficient_ref[2, y] = kappa - flow_y
        coefficient_ref[3, y] = kappa + flow_y
        coefficient_ref[4, y] = jnp.where(lane == NZ - 1, 0.0, kappa - flow_z)
        coefficient_ref[5, y] = jnp.where(lane == 0, 0.0, kappa + flow_z)
        real_first = first + 6.0 * kappa
        real_second = second + 6.0 * kappa
        over_first = weight / (real_first * real_first + turn * turn)
        over_second = weight / (real_second * real_second + turn * turn)
        coefficient_ref[6, y] = real_first * over_first
        coefficient_ref[7, y] = turn * over_first
        coefficient_ref[8, y] = real_second * over_second
        return carry

    lax.fori_loop(0, WIDE, prepare, 0, unroll=2)


def solve_slot(spectrum_ref, coefficient_ref, sent_ref, source, even, odd):
    def scale(y, one, two):
        a, b, c = coefficient_ref[6, y], coefficient_ref[7, y], coefficient_ref[8, y]
        return a * one + b * two, c * two - b * one

    blank = jnp.zeros((2, NX, NZ), F32)
    even[0] = blank
    even[WIDE + 1] = blank
    for member in range(MEMBERS):
        for row in range(WIDE_EACH):
            at = member * NX * 2 * WIDE_EACH + row
            y = member * WIDE_EACH + row
            one = spectrum_ref[pl.ds(at, NX, stride=2 * WIDE_EACH), :]
            two = spectrum_ref[pl.ds(at + WIDE_EACH, NX, stride=2 * WIDE_EACH), :]
            source[y, 0] = one
            source[y, 1] = two
            even[y + 1, 0], even[y + 1, 1] = scale(y, one, two)

    for sweep in range(SWEEPS):
        now, later = (even, odd) if sweep % 2 == 0 else (odd, even)
        begin = (sweep + 1) // 2 * 2
        end = WIDE - begin

        def row(y, carry):
            south, here = carry
            north = (now[y + 2, 0], now[y + 2, 1])
            totals = []
            for part in range(2):
                mid = here[part]
                total = source[y, part]
                total += coefficient_ref[0, y] * pltpu.roll(mid, NX - 1, 0)
                total += coefficient_ref[1, y] * pltpu.roll(mid, 1, 0)
                total += coefficient_ref[2, y] * north[part] + coefficient_ref[3, y] * south[part]
                total += coefficient_ref[4, y] * pltpu.roll(mid, NZ - 1, 1)
                total += coefficient_ref[5, y] * pltpu.roll(mid, 1, 1)
                totals.append(total)
            later[y + 1, 0], later[y + 1, 1] = scale(y, *totals)
            return here, north

        start = tuple((now[begin + k, 0], now[begin + k, 1]) for k in range(2))
        lax.fori_loop(begin, end, row, start, unroll=4)

    field = even if SWEEPS % 2 == 0 else odd
    for member in range(MEMBERS):
        for row in range(EACH):
            for part in range(2):
                at = member * NX * 2 * EACH + part * EACH + row
                sent_ref[pl.ds(at, NX, stride=2 * EACH), :] = field[HALO + member * EACH + row + 1, part]


def call(kernel, out_shape, in_specs, scratch=(), flops=1_000_000, moved=2_000_000):
    return pl.pallas_call(
        kernel,
        out_shape=out_shape,
        in_specs=in_specs,
        out_specs=jax.tree.map(lambda _: VMEM, out_shape),
        scratch_shapes=scratch,
        cost_estimate=pl.CostEstimate(flops=flops, bytes_accessed=moved, transcendentals=0),
        compiler_params=pltpu.CompilerParams(vmem_limit_bytes=GRANT),
    )


def shape(*dims):
    return jax.ShapeDtypeStruct(dims, F32)


def exchange(value, axes):
    return lax.all_to_all(value, axes, split_axis=0, concat_axis=0, tiled=True)


def local(iterate, forcing, start_field, classes, open_mask, diffusivity, drift):
    forward, back, shift = tables()
    iterate = iterate.reshape(LOCAL, NY, NZ)
    forcing = forcing.reshape(LOCAL, NY, NZ)
    start_field = start_field.reshape(NY, NZ)
    classes = classes.reshape(NY, NZ)
    open_mask = open_mask.reshape(NY, NZ)

    cells = lax.optimization_barrier(jnp.where(open_mask == 1, classes, SOLID))
    masked = iterate * (cells != SOLID).astype(F32)
    per_class = jnp.concatenate([diffusivity[None], drift])
    up = [(i, i + 1) for i in range(NX - 1)]
    down = [(j, i) for i, j in up]
    west = lax.ppermute(masked, SPACE, up)
    east = lax.ppermute(masked, SPACE, down)
    arrived = lax.ppermute(masked[LOCAL - 1], TM, [(i, i + 1) for i in range(GROUPS - 1)])

    plane = cells
    cells = jnp.pad(cells, ((HALO, HALO), (0, 0)), constant_values=SOLID)
    cells = lax.dynamic_slice_in_dim(cells, lax.axis_index(("yh", "zh")) * SPAN, WIDE, 0)
    cells = cells.reshape(1, 1, WIDE, NZ)
    for hop in range(2):
        other = lax.ppermute(cells, "yl", [(i, i ^ (hop + 1)) for i in range(4)])
        upper = (lax.axis_index("yl") & (hop + 1)) != 0
        cells = jnp.concatenate([jnp.where(upper, other, cells), jnp.where(upper, cells, other)], axis=0)
    column = lax.axis_index("x")
    held = [cells]
    for apart in range(1, 4):
        held.append(lax.ppermute(cells, "x", [(i, i ^ apart) for i in range(4)]))
    cells = jnp.concatenate(
        [lax.select_n(column ^ at, *held) for at in range(4)],
        axis=1,
    )
    cells = cells.reshape(NX * WIDE, NZ)

    first = (lax.axis_index(TM) == 0).astype(jnp.int32).reshape(1)
    part, side = call(
        local_terms,
        (shape(LOCAL, NY, NZ), shape(3, NY, NZ)),
        [VMEM] * 4 + [SMEM] * 2,
    )(masked, forcing, plane, start_field, per_class, first)
    residual, sent = call(
        finish_residual,
        (shape(LOCAL, NY, NZ), shape(QUARTERS * WIDE * LOCAL, NZ)),
        [VMEM] * 5,
    )(part, side, east, west, arrived)

    steps = exchange(sent, TM).reshape(GROUPS, WIDE_EACH, LOCAL, NZ)
    sent = call(to_frequencies, shape(SLOTS * 2 * WIDE_EACH, NZ), [VMEM] * 2)(steps, jnp.asarray(forward))
    spectrum = exchange(sent.reshape(SLOTS, 1, 2 * WIDE_EACH * NZ), BLOCK).reshape(SLOTS * 2 * WIDE_EACH, NZ)
    mine = lax.dynamic_slice_in_dim(jnp.asarray(shift), lax.axis_index(BLOCK), 1, 0).reshape(4)
    coefficient = call(prepare_slot, shape(9, WIDE, NX, NZ), [VMEM] + [SMEM] * 2)(cells, per_class, mine)
    sent = call(
        solve_slot,
        shape(SLOTS * 2 * EACH, NZ),
        [VMEM] * 2,
        scratch=[
            pltpu.VMEM((WIDE, 2, NX, NZ), F32),
            pltpu.VMEM((WIDE + 2, 2, NX, NZ), F32),
            pltpu.VMEM((WIDE + 2, 2, NX, NZ), F32),
        ],
    )(spectrum, coefficient)
    solved = exchange(sent, BLOCK)
    sent = call(to_steps, shape(GROUPS, EACH, LOCAL, NZ), [VMEM] * 2)(solved, jnp.asarray(back))
    rows = exchange(sent.reshape(GROUPS * EACH * LOCAL, NZ), TM)
    corrected = call(to_grid, shape(LOCAL, NY, NZ), [VMEM])(rows)
    grid = (LOCAL, 1, NY, NZ)
    return residual.reshape(grid), corrected.reshape(grid)


def solution(mesh):
    fine = Mesh(mesh.devices.reshape(2, 2, 4, 2, 4, 4), AXES)
    big = P(TM, SPACE, None, None)
    plane = P(SPACE, None, None)

    return jax.shard_map(
        local,
        mesh=fine,
        in_specs=(big, big, plane, plane, plane, P(), P()),
        out_specs=(big, big),
        check_vma=False,
    )
```

```python
import jax
import jax.numpy as jnp
import numpy as np
from jax import lax
from jax.experimental import pallas as pl
from jax.experimental.pallas import tpu as pltpu
from jax.sharding import Mesh
from jax.sharding import PartitionSpec as P


SWEEPS = 4
ALPHA = 0.1
STEPS = 256
GROUPS = 32
LOCAL = STEPS // GROUPS
NX, NY, NZ = 16, 128, 128
QUARTERS = 4
MEMBERS = GROUPS // QUARTERS
SPAN = NY // QUARTERS
HALO = SWEEPS
WIDE = SPAN + 2 * HALO
WIDE_EACH = WIDE // MEMBERS
EACH = SPAN // MEMBERS
SLOTS = STEPS // 2
CLASSES = 8
SOLID = CLASSES

AXES = ("yh", "zh", "zl", "core", "yl", "x")
TM = ("yh", "zh", "zl", "core")
SPACE = ("yl", "x")
BLOCK = ("zl", "core", "yl", "x")

GRANT = 16 << 20
VMEM = pl.BlockSpec(memory_space=pltpu.VMEM)
SMEM = pl.BlockSpec(memory_space=pltpu.SMEM)
F32 = jnp.float32


def tables():
    n = np.arange(STEPS, dtype=np.float64)
    k = np.arange(SLOTS, dtype=np.float64)
    ramp = ALPHA ** (n / STEPS)
    angle = 2.0 * np.pi * ((n[None, :] * k[:, None]) % STEPS) / STEPS
    cosine, sine = np.cos(angle), np.sin(angle)
    alternate = np.where(np.arange(STEPS) % 2 == 0, 1.0, -1.0)
    real, imag = cosine.copy(), -sine
    imag[0] = alternate
    forward = np.concatenate([real, imag], axis=0) * ramp
    real, imag = 2.0 * cosine, -2.0 * sine
    real[0] = 1.0
    imag[0] = alternate
    back = np.concatenate([real, imag], axis=0) / (ramp * STEPS)
    root = ALPHA ** (1.0 / STEPS)
    base = 2.0 * np.pi * k / STEPS
    first = 1.0 - root * np.cos(base)
    second = first.copy()
    second[0] = 1.0 + root
    turn = root * np.sin(base)
    shift = np.stack([first, second, turn, np.zeros_like(turn)], axis=1)
    return forward.astype(np.float32), back.T.astype(np.float32).copy(), shift.astype(np.float32)


def look_up(classes, class_ref):
    found = [jnp.full(classes.shape, class_ref[kind, 0], F32) for kind in range(4)]
    for level in range(1, CLASSES):
        match = classes == level
        found = [jnp.where(match, class_ref[kind, level], found[kind]) for kind in range(4)]
    kappa, *tilts = found
    return jnp.where(classes == SOLID, 0.0, 1.0), kappa, [kappa * tilt for tilt in tilts]


def local_terms(masked_ref, forcing_ref, cells_ref, class_ref, part_ref, side_ref):
    weight, kappa, (flow_x, flow_y, flow_z) = look_up(cells_ref[...], class_ref)
    row = lax.broadcasted_iota(jnp.int32, (NY, NZ), 0)
    lane = lax.broadcasted_iota(jnp.int32, (NY, NZ), 1)
    side_ref[0] = weight * (kappa - flow_x)
    side_ref[1] = weight * (kappa + flow_x)
    side_ref[2] = weight
    north = jnp.where(row == NY - 1, 0.0, weight * (kappa - flow_y))
    south = jnp.where(row == 0, 0.0, weight * (kappa + flow_y))
    upper = jnp.where(lane == NZ - 1, 0.0, weight * (kappa - flow_z))
    lower = jnp.where(lane == 0, 0.0, weight * (kappa + flow_z))
    middle = 1.0 + 6.0 * kappa
    for n in range(LOCAL):
        here = masked_ref[n]
        total = weight * forcing_ref[n] - middle * here
        total += north * pltpu.roll(here, NY - 1, 0) + south * pltpu.roll(here, 1, 0)
        total += upper * pltpu.roll(here, NZ - 1, 1) + lower * pltpu.roll(here, 1, 1)
        if n:
            total += masked_ref[n - 1]
        part_ref[n] = total


def finish_residual(part_ref, side_ref, east_ref, west_ref, start_ref, arrived_ref, first_ref, residual_ref, sent_ref):
    east, west, weight = side_ref[0], side_ref[1], side_ref[2]
    begins = first_ref[0]
    step_before = weight * jnp.where(begins == 1, start_ref[...], arrived_ref[...])
    for n in range(LOCAL):
        total = part_ref[n] + east * east_ref[n] + west * west_ref[n]
        if n == 0:
            total += step_before
        residual_ref[n] = total
        for quarter in range(QUARTERS):
            low = max(quarter * SPAN - HALO, 0)
            high = min((quarter + 1) * SPAN + HALO, NY)
            at = quarter * WIDE + low - (quarter * SPAN - HALO)
            sent_ref[pl.ds(at * LOCAL + n, high - low, stride=LOCAL), :] = total[low:high]
    outside = jnp.zeros((HALO * LOCAL, NZ), F32)
    sent_ref[0 : HALO * LOCAL, :] = outside
    sent_ref[(QUARTERS * WIDE - HALO) * LOCAL :, :] = outside


def to_frequencies(steps_ref, table_ref, sent_ref):
    fields = [steps_ref[:, row].reshape(STEPS, NZ) for row in range(WIDE_EACH)]
    spectrum = jnp.dot(
        table_ref[...],
        jnp.concatenate(fields, axis=1),
        precision=lax.Precision.HIGHEST,
        preferred_element_type=F32,
    )
    for row in range(WIDE_EACH):
        columns = spectrum[:, row * NZ : (row + 1) * NZ]
        for part in range(2):
            rows = columns[part * SLOTS : (part + 1) * SLOTS]
            sent_ref[pl.ds(part * WIDE_EACH + row, SLOTS, stride=2 * WIDE_EACH), :] = rows


def to_steps(slots_ref, table_ref, sent_ref):
    columns = []
    for row in range(EACH):
        parts = [slots_ref[pl.ds(part * EACH + row, SLOTS, stride=2 * EACH), :] for part in range(2)]
        columns.append(jnp.concatenate(parts, axis=0))
    steps = jnp.dot(
        table_ref[...],
        jnp.concatenate(columns, axis=1),
        precision=lax.Precision.HIGHEST,
        preferred_element_type=F32,
    )
    for row in range(EACH):
        sent_ref[:, row] = steps[:, row * NZ : (row + 1) * NZ].reshape(GROUPS, LOCAL, NZ)


def to_grid(rows_ref, out_ref):
    for n in range(LOCAL):
        out_ref[n] = rows_ref[pl.ds(n, NY, stride=LOCAL), :]


def prepare_slot(cells_ref, class_ref, shift_ref, coefficient_ref):
    sublane = lax.broadcasted_iota(jnp.int32, (NX // 2, NZ), 0)
    lane = lax.broadcasted_iota(jnp.int32, (NX // 2, NZ), 1)
    first, second, turn = shift_ref[0], shift_ref[1], shift_ref[2]

    def prepare(y, carry):
        for odd in range(2):
            classes = cells_ref[pl.ds(y + odd * WIDE, NX // 2, stride=2 * WIDE), :]
            weight, kappa, (flow_x, flow_y, flow_z) = look_up(classes, class_ref)
            east, west = kappa - flow_x, kappa + flow_x
            if odd:
                east = jnp.where(sublane == NX // 2 - 1, 0.0, east)
            else:
                west = jnp.where(sublane == 0, 0.0, west)
            coefficient_ref[0, y, odd] = east
            coefficient_ref[1, y, odd] = west
            coefficient_ref[2, y, odd] = kappa - flow_y
            coefficient_ref[3, y, odd] = kappa + flow_y
            coefficient_ref[4, y, odd] = jnp.where(lane == NZ - 1, 0.0, kappa - flow_z)
            coefficient_ref[5, y, odd] = jnp.where(lane == 0, 0.0, kappa + flow_z)
            real_first = first + 6.0 * kappa
            real_second = second + 6.0 * kappa
            over_first = weight / (real_first * real_first + turn * turn)
            over_second = weight / (real_second * real_second + turn * turn)
            coefficient_ref[6, y, odd] = real_first * over_first
            coefficient_ref[7, y, odd] = turn * over_first
            coefficient_ref[8, y, odd] = real_second * over_second
        return carry

    lax.fori_loop(0, WIDE, prepare, 0, unroll=2)


def solve_slot(spectrum_ref, coefficient_ref, sent_ref, source, even, odd):
    tile = NX // 2

    def scale(y, half, one, two):
        a, b, c = (coefficient_ref[kind, y, half] for kind in (6, 7, 8))
        return a * one + b * two, c * two - b * one

    blank = jnp.zeros((2, 2, tile, NZ), F32)
    for field in (even, odd):
        field[0] = blank
        field[WIDE + 1] = blank
    rows = 2 * WIDE_EACH
    for member in range(MEMBERS):
        for row in range(WIDE_EACH):
            y = member * WIDE_EACH + row
            for half in range(2):
                at = (member * NX + half) * rows + row
                one = spectrum_ref[pl.ds(at, tile, stride=2 * rows), :]
                two = spectrum_ref[pl.ds(at + WIDE_EACH, tile, stride=2 * rows), :]
                source[y, 0, half] = one
                source[y, 1, half] = two
                even[y + 1, 0, half], even[y + 1, 1, half] = scale(y, half, one, two)

    for sweep in range(SWEEPS):
        now, later = (even, odd) if sweep % 2 == 0 else (odd, even)
        begin = HALO if sweep == SWEEPS - 1 else 0
        end = WIDE - begin

        def row(y, carry):
            south, here = carry
            north = tuple(tuple(now[y + 2, part, half] for half in range(2)) for part in range(2))
            for half in range(2):
                totals = []
                for part in range(2):
                    mid, across = here[part][half], here[part][1 - half]
                    east = pltpu.roll(across, tile - 1, 0) if half else across
                    west = across if half else pltpu.roll(across, 1, 0)
                    total = source[y, part, half]
                    total += coefficient_ref[0, y, half] * east + coefficient_ref[1, y, half] * west
                    total += coefficient_ref[2, y, half] * north[part][half]
                    total += coefficient_ref[3, y, half] * south[part][half]
                    total += coefficient_ref[4, y, half] * pltpu.roll(mid, NZ - 1, 1)
                    total += coefficient_ref[5, y, half] * pltpu.roll(mid, 1, 1)
                    totals.append(total)
                later[y + 1, 0, half], later[y + 1, 1, half] = scale(y, half, *totals)
            return here, north

        start = tuple(
            tuple(tuple(now[begin + k, part, half] for half in range(2)) for part in range(2)) for k in range(2)
        )
        lax.fori_loop(begin, end, row, start, unroll=8)

    field = even if SWEEPS % 2 == 0 else odd
    rows = 2 * EACH
    for member in range(MEMBERS):
        for row in range(EACH):
            for part in range(2):
                for half in range(2):
                    at = (member * NX + half) * rows + part * EACH + row
                    value = field[HALO + member * EACH + row + 1, part, half]
                    sent_ref[pl.ds(at, tile, stride=2 * rows), :] = value


def call(kernel, out_shape, in_specs, scratch=(), flops=1_000_000, moved=2_000_000):
    return pl.pallas_call(
        kernel,
        out_shape=out_shape,
        in_specs=in_specs,
        out_specs=jax.tree.map(lambda _: VMEM, out_shape),
        scratch_shapes=scratch,
        cost_estimate=pl.CostEstimate(flops=flops, bytes_accessed=moved, transcendentals=0),
        compiler_params=pltpu.CompilerParams(vmem_limit_bytes=GRANT),
    )


def shape(*dims):
    return jax.ShapeDtypeStruct(dims, F32)


def exchange(value, axes):
    return lax.all_to_all(value, axes, split_axis=0, concat_axis=0, tiled=True)


def local(iterate, forcing, start_field, classes, open_mask, diffusivity, drift):
    forward, back, shift = tables()
    iterate = iterate.reshape(LOCAL, NY, NZ)
    forcing = forcing.reshape(LOCAL, NY, NZ)
    start_field = start_field.reshape(NY, NZ)
    classes = classes.reshape(NY, NZ)
    open_mask = open_mask.reshape(NY, NZ)

    cells = lax.optimization_barrier(jnp.where(open_mask == 1, classes, SOLID))
    masked = iterate * (cells != SOLID).astype(F32)
    per_class = jnp.concatenate([diffusivity[None], drift])
    up = [(i, i + 1) for i in range(NX - 1)]
    down = [(j, i) for i, j in up]
    west = lax.ppermute(masked, SPACE, up)
    east = lax.ppermute(masked, SPACE, down)
    arrived = lax.ppermute(masked[LOCAL - 1], TM, [(i, i + 1) for i in range(GROUPS - 1)])

    plane = cells
    cells = jnp.pad(cells, ((HALO, HALO), (0, 0)), constant_values=SOLID)
    cells = lax.dynamic_slice_in_dim(cells, lax.axis_index(("yh", "zh")) * SPAN, WIDE, 0)
    cells = cells.reshape(1, 1, WIDE, NZ)
    for axis, dim, bit in (("yl", 0, 1), ("yl", 0, 2), ("x", 1, 1), ("x", 1, 2)):
        other = lax.ppermute(cells, axis, [(i, i ^ bit) for i in range(4)])
        upper = (lax.axis_index(axis) & bit) != 0
        pair = [jnp.where(upper, other, cells), jnp.where(upper, cells, other)]
        cells = jnp.concatenate(pair, axis=dim)
    cells = cells.reshape(NX * WIDE, NZ)

    part, side = call(
        local_terms,
        (shape(LOCAL, NY, NZ), shape(3, NY, NZ)),
        [VMEM] * 3 + [SMEM],
    )(masked, forcing, plane, per_class)
    first = (lax.axis_index(TM) == 0).astype(jnp.int32).reshape(1)
    residual, sent = call(
        finish_residual,
        (shape(LOCAL, NY, NZ), shape(QUARTERS * WIDE * LOCAL, NZ)),
        [VMEM] * 6 + [SMEM],
    )(part, side, east, west, start_field, arrived, first)

    steps = exchange(sent, TM).reshape(GROUPS, WIDE_EACH, LOCAL, NZ)
    sent = call(to_frequencies, shape(SLOTS * 2 * WIDE_EACH, NZ), [VMEM] * 2)(steps, jnp.asarray(forward))
    spectrum = exchange(sent.reshape(SLOTS, 1, 2 * WIDE_EACH * NZ), BLOCK).reshape(SLOTS * 2 * WIDE_EACH, NZ)
    mine = lax.dynamic_slice_in_dim(jnp.asarray(shift), lax.axis_index(BLOCK), 1, 0).reshape(4)
    coefficient = call(prepare_slot, shape(9, WIDE, 2, NX // 2, NZ), [VMEM] + [SMEM] * 2)(cells, per_class, mine)
    sent = call(
        solve_slot,
        shape(SLOTS * 2 * EACH, NZ),
        [VMEM] * 2,
        scratch=[
            pltpu.VMEM((WIDE, 2, 2, NX // 2, NZ), F32),
            pltpu.VMEM((WIDE + 2, 2, 2, NX // 2, NZ), F32),
            pltpu.VMEM((WIDE + 2, 2, 2, NX // 2, NZ), F32),
        ],
    )(spectrum, coefficient)
    solved = exchange(sent, BLOCK)
    sent = call(to_steps, shape(GROUPS, EACH, LOCAL, NZ), [VMEM] * 2)(solved, jnp.asarray(back))
    rows = exchange(sent.reshape(GROUPS * EACH * LOCAL, NZ), TM)
    corrected = call(to_grid, shape(LOCAL, NY, NZ), [VMEM])(rows)
    grid = (LOCAL, 1, NY, NZ)
    return residual.reshape(grid), corrected.reshape(grid)


def solution(mesh):
    fine = Mesh(mesh.devices.reshape(2, 2, 4, 2, 4, 4), AXES)
    big = P(TM, SPACE, None, None)
    plane = P(SPACE, None, None)

    return jax.shard_map(
        local,
        mesh=fine,
        in_specs=(big, big, plane, plane, plane, P(), P()),
        out_specs=(big, big),
        check_vma=False,
    )
```

```python
import jax
import jax.numpy as jnp
import numpy as np
from jax import lax
from jax.experimental import pallas as pl
from jax.experimental.pallas import tpu as pltpu
from jax.sharding import Mesh
from jax.sharding import PartitionSpec as P


SWEEPS = 4
ALPHA = 0.1
STEPS = 256
GROUPS = 32
LOCAL = STEPS // GROUPS
NX, NY, NZ = 16, 128, 128
QUARTERS = 4
MEMBERS = GROUPS // QUARTERS
SPAN = NY // QUARTERS
HALO = SWEEPS
WIDE = SPAN + 2 * HALO
WIDE_EACH = WIDE // MEMBERS
EACH = SPAN // MEMBERS
SLOTS = STEPS // 2
CLASSES = 8
SOLID = CLASSES

AXES = ("yh", "zh", "zl", "core", "yl", "x")
TM = ("yh", "zh", "zl", "core")
SPACE = ("yl", "x")
BLOCK = ("zl", "core", "yl", "x")

GRANT = 16 << 20
VMEM = pl.BlockSpec(memory_space=pltpu.VMEM)
SMEM = pl.BlockSpec(memory_space=pltpu.SMEM)
F32 = jnp.float32


def tables():
    n = np.arange(STEPS, dtype=np.float64)
    k = np.arange(SLOTS, dtype=np.float64)
    ramp = ALPHA ** (n / STEPS)
    angle = 2.0 * np.pi * ((n[None, :] * k[:, None]) % STEPS) / STEPS
    cosine, sine = np.cos(angle), np.sin(angle)
    alternate = np.where(np.arange(STEPS) % 2 == 0, 1.0, -1.0)
    real, imag = cosine.copy(), -sine
    imag[0] = alternate
    forward = np.concatenate([real, imag], axis=0) * ramp
    real, imag = 2.0 * cosine, -2.0 * sine
    real[0] = 1.0
    imag[0] = alternate
    back = np.concatenate([real, imag], axis=0) / (ramp * STEPS)
    root = ALPHA ** (1.0 / STEPS)
    base = 2.0 * np.pi * k / STEPS
    first = 1.0 - root * np.cos(base)
    second = first.copy()
    second[0] = 1.0 + root
    turn = root * np.sin(base)
    shift = np.stack([first, second, turn, np.zeros_like(turn)], axis=1)
    return forward.astype(np.float32), back.T.astype(np.float32).copy(), shift.astype(np.float32)


def look_up(classes, class_ref):
    found = [jnp.full(classes.shape, class_ref[kind, 0], F32) for kind in range(4)]
    for level in range(1, CLASSES):
        match = classes == level
        found = [jnp.where(match, class_ref[kind, level], found[kind]) for kind in range(4)]
    kappa, *tilts = found
    return jnp.where(classes == SOLID, 0.0, 1.0), kappa, [kappa * tilt for tilt in tilts]


def local_terms(masked_ref, forcing_ref, cells_ref, class_ref, part_ref, side_ref):
    weight, kappa, (flow_x, flow_y, flow_z) = look_up(cells_ref[...], class_ref)
    row = lax.broadcasted_iota(jnp.int32, (NY, NZ), 0)
    lane = lax.broadcasted_iota(jnp.int32, (NY, NZ), 1)
    side_ref[0] = weight * (kappa - flow_x)
    side_ref[1] = weight * (kappa + flow_x)
    side_ref[2] = weight
    north = jnp.where(row == NY - 1, 0.0, weight * (kappa - flow_y))
    south = jnp.where(row == 0, 0.0, weight * (kappa + flow_y))
    upper = jnp.where(lane == NZ - 1, 0.0, weight * (kappa - flow_z))
    lower = jnp.where(lane == 0, 0.0, weight * (kappa + flow_z))
    middle = 1.0 + 6.0 * kappa
    for n in range(LOCAL):
        here = masked_ref[n]
        total = weight * forcing_ref[n] - middle * here
        total += north * pltpu.roll(here, NY - 1, 0) + south * pltpu.roll(here, 1, 0)
        total += upper * pltpu.roll(here, NZ - 1, 1) + lower * pltpu.roll(here, 1, 1)
        if n:
            total += masked_ref[n - 1]
        part_ref[n] = total


def finish_residual(part_ref, side_ref, east_ref, west_ref, start_ref, arrived_ref, first_ref, residual_ref, sent_ref):
    east, west, weight = side_ref[0], side_ref[1], side_ref[2]
    begins = first_ref[0]
    step_before = weight * jnp.where(begins == 1, start_ref[...], arrived_ref[...])
    for n in range(LOCAL):
        total = part_ref[n] + east * east_ref[n] + west * west_ref[n]
        if n == 0:
            total += step_before
        residual_ref[n] = total
        for quarter in range(QUARTERS):
            low = max(quarter * SPAN - HALO, 0)
            high = min((quarter + 1) * SPAN + HALO, NY)
            at = quarter * WIDE + low - (quarter * SPAN - HALO)
            sent_ref[pl.ds(at * LOCAL + n, high - low, stride=LOCAL), :] = total[low:high]
    outside = jnp.zeros((HALO * LOCAL, NZ), F32)
    sent_ref[0 : HALO * LOCAL, :] = outside
    sent_ref[(QUARTERS * WIDE - HALO) * LOCAL :, :] = outside


def to_frequencies(steps_ref, table_ref, sent_ref):
    fields = [steps_ref[:, row].reshape(STEPS, NZ) for row in range(WIDE_EACH)]
    spectrum = jnp.dot(
        table_ref[...],
        jnp.concatenate(fields, axis=1),
        precision=lax.Precision.HIGHEST,
        preferred_element_type=F32,
    )
    for row in range(WIDE_EACH):
        columns = spectrum[:, row * NZ : (row + 1) * NZ]
        for part in range(2):
            rows = columns[part * SLOTS : (part + 1) * SLOTS]
            sent_ref[pl.ds(part * WIDE_EACH + row, SLOTS, stride=2 * WIDE_EACH), :] = rows


def to_steps(slots_ref, table_ref, sent_ref):
    columns = []
    for row in range(EACH):
        parts = [slots_ref[pl.ds(part * EACH + row, SLOTS, stride=2 * EACH), :] for part in range(2)]
        columns.append(jnp.concatenate(parts, axis=0))
    steps = jnp.dot(
        table_ref[...],
        jnp.concatenate(columns, axis=1),
        precision=lax.Precision.HIGHEST,
        preferred_element_type=F32,
    )
    for row in range(EACH):
        sent_ref[:, row] = steps[:, row * NZ : (row + 1) * NZ].reshape(GROUPS, LOCAL, NZ)


def to_grid(rows_ref, out_ref):
    for n in range(LOCAL):
        out_ref[n] = rows_ref[pl.ds(n, NY, stride=LOCAL), :]


def prepare_slot(cells_ref, class_ref, shift_ref, coefficient_ref):
    sublane = lax.broadcasted_iota(jnp.int32, (NX // 2, NZ), 0)
    lane = lax.broadcasted_iota(jnp.int32, (NX // 2, NZ), 1)
    first, second, turn = shift_ref[0], shift_ref[1], shift_ref[2]

    def prepare(y, carry):
        for odd in range(2):
            classes = cells_ref[pl.ds(y + odd * WIDE, NX // 2, stride=2 * WIDE), :]
            weight, kappa, (flow_x, flow_y, flow_z) = look_up(classes, class_ref)
            east, west = kappa - flow_x, kappa + flow_x
            if odd:
                east = jnp.where(sublane == NX // 2 - 1, 0.0, east)
            else:
                west = jnp.where(sublane == 0, 0.0, west)
            coefficient_ref[0, y, odd] = east
            coefficient_ref[1, y, odd] = west
            coefficient_ref[2, y, odd] = kappa - flow_y
            coefficient_ref[3, y, odd] = kappa + flow_y
            coefficient_ref[4, y, odd] = jnp.where(lane == NZ - 1, 0.0, kappa - flow_z)
            coefficient_ref[5, y, odd] = jnp.where(lane == 0, 0.0, kappa + flow_z)
            real_first = first + 6.0 * kappa
            real_second = second + 6.0 * kappa
            over_first = weight / (real_first * real_first + turn * turn)
            over_second = weight / (real_second * real_second + turn * turn)
            coefficient_ref[6, y, odd] = real_first * over_first
            coefficient_ref[7, y, odd] = turn * over_first
            coefficient_ref[8, y, odd] = real_second * over_second
        return carry

    lax.fori_loop(0, WIDE, prepare, 0, unroll=2)


def solve_slot(spectrum_ref, coefficient_ref, sent_ref, source, even, odd):
    tile = NX // 2

    def scale(y, half, one, two):
        a, b, c = (coefficient_ref[kind, y, half] for kind in (6, 7, 8))
        return a * one + b * two, c * two - b * one

    blank = jnp.zeros((2, 2, tile, NZ), F32)
    for field in (even, odd):
        field[0] = blank
        field[WIDE + 1] = blank
    rows = 2 * WIDE_EACH
    for member in range(MEMBERS):
        for row in range(WIDE_EACH):
            y = member * WIDE_EACH + row
            for half in range(2):
                at = (member * NX + half) * rows + row
                one = spectrum_ref[pl.ds(at, tile, stride=2 * rows), :]
                two = spectrum_ref[pl.ds(at + WIDE_EACH, tile, stride=2 * rows), :]
                source[y, 0, half] = one
                source[y, 1, half] = two
                even[y + 1, 0, half], even[y + 1, 1, half] = scale(y, half, one, two)

    for sweep in range(SWEEPS):
        now, later = (even, odd) if sweep % 2 == 0 else (odd, even)
        begin = HALO if sweep == SWEEPS - 1 else 0
        end = WIDE - begin

        def row(y, carry):
            south, here = carry
            north = tuple(tuple(now[y + 2, part, half] for half in range(2)) for part in range(2))
            for half in range(2):
                totals = []
                for part in range(2):
                    mid, across = here[part][half], here[part][1 - half]
                    east = pltpu.roll(across, tile - 1, 0) if half else across
                    west = across if half else pltpu.roll(across, 1, 0)
                    total = source[y, part, half]
                    total += coefficient_ref[0, y, half] * east + coefficient_ref[1, y, half] * west
                    total += coefficient_ref[2, y, half] * north[part][half]
                    total += coefficient_ref[3, y, half] * south[part][half]
                    total += coefficient_ref[4, y, half] * pltpu.roll(mid, NZ - 1, 1)
                    total += coefficient_ref[5, y, half] * pltpu.roll(mid, 1, 1)
                    totals.append(total)
                later[y + 1, 0, half], later[y + 1, 1, half] = scale(y, half, *totals)
            return here, north

        start = tuple(
            tuple(tuple(now[begin + k, part, half] for half in range(2)) for part in range(2)) for k in range(2)
        )
        lax.fori_loop(begin, end, row, start, unroll=8)

    field = even if SWEEPS % 2 == 0 else odd
    rows = 2 * EACH
    for member in range(MEMBERS):
        for row in range(EACH):
            for part in range(2):
                for half in range(2):
                    at = (member * NX + half) * rows + part * EACH + row
                    value = field[HALO + member * EACH + row + 1, part, half]
                    sent_ref[pl.ds(at, tile, stride=2 * rows), :] = value


def call(kernel, out_shape, in_specs, scratch=(), flops=1_000_000, moved=2_000_000):
    return pl.pallas_call(
        kernel,
        out_shape=out_shape,
        in_specs=in_specs,
        out_specs=jax.tree.map(lambda _: VMEM, out_shape),
        scratch_shapes=scratch,
        cost_estimate=pl.CostEstimate(flops=flops, bytes_accessed=moved, transcendentals=0),
        compiler_params=pltpu.CompilerParams(vmem_limit_bytes=GRANT),
    )


def shape(*dims):
    return jax.ShapeDtypeStruct(dims, F32)


def exchange(value, axes):
    return lax.all_to_all(value, axes, split_axis=0, concat_axis=0, tiled=True)


def local(iterate, forcing, start_field, classes, open_mask, diffusivity, drift):
    forward, back, shift = tables()
    iterate = iterate.reshape(LOCAL, NY, NZ)
    forcing = forcing.reshape(LOCAL, NY, NZ)
    start_field = start_field.reshape(NY, NZ)
    classes = classes.reshape(NY, NZ)
    open_mask = open_mask.reshape(NY, NZ)

    cells = lax.optimization_barrier(jnp.where(open_mask == 1, classes, SOLID))
    masked = iterate * (cells != SOLID).astype(F32)
    per_class = jnp.concatenate([diffusivity[None], drift])
    up = [(i, i + 1) for i in range(NX - 1)]
    down = [(j, i) for i, j in up]
    west = lax.ppermute(masked, SPACE, up)
    east = lax.ppermute(masked, SPACE, down)
    arrived = lax.ppermute(masked[LOCAL - 1], TM, [(i, i + 1) for i in range(GROUPS - 1)])

    plane = cells
    cells = jnp.pad(cells, ((HALO, HALO), (0, 0)), constant_values=SOLID)
    cells = lax.dynamic_slice_in_dim(cells, lax.axis_index(("yh", "zh")) * SPAN, WIDE, 0)
    cells = cells.reshape(1, 1, WIDE, NZ)
    held = [cells]
    for apart in range(1, 4):
        held.append(lax.ppermute(cells, "yl", [(i, i ^ apart) for i in range(4)]))
    mine_y = lax.axis_index("yl")
    cells = jnp.concatenate([lax.select_n(mine_y ^ at, *held) for at in range(4)], axis=0)
    for hop in range(2):
        other = lax.ppermute(cells, "x", [(i, i ^ (hop + 1)) for i in range(4)])
        upper = (lax.axis_index("x") & (hop + 1)) != 0
        cells = jnp.concatenate([jnp.where(upper, other, cells), jnp.where(upper, cells, other)], axis=1)
    cells = cells.reshape(NX * WIDE, NZ)

    part, side = call(
        local_terms,
        (shape(LOCAL, NY, NZ), shape(3, NY, NZ)),
        [VMEM] * 3 + [SMEM],
    )(masked, forcing, plane, per_class)
    first = (lax.axis_index(TM) == 0).astype(jnp.int32).reshape(1)
    residual, sent = call(
        finish_residual,
        (shape(LOCAL, NY, NZ), shape(QUARTERS * WIDE * LOCAL, NZ)),
        [VMEM] * 6 + [SMEM],
    )(part, side, east, west, start_field, arrived, first)

    steps = exchange(sent, TM).reshape(GROUPS, WIDE_EACH, LOCAL, NZ)
    sent = call(to_frequencies, shape(SLOTS * 2 * WIDE_EACH, NZ), [VMEM] * 2)(steps, jnp.asarray(forward))
    spectrum = exchange(sent.reshape(SLOTS, 1, 2 * WIDE_EACH * NZ), BLOCK).reshape(SLOTS * 2 * WIDE_EACH, NZ)
    mine = lax.dynamic_slice_in_dim(jnp.asarray(shift), lax.axis_index(BLOCK), 1, 0).reshape(4)
    coefficient = call(prepare_slot, shape(9, WIDE, 2, NX // 2, NZ), [VMEM] + [SMEM] * 2)(cells, per_class, mine)
    sent = call(
        solve_slot,
        shape(SLOTS * 2 * EACH, NZ),
        [VMEM] * 2,
        scratch=[
            pltpu.VMEM((WIDE, 2, 2, NX // 2, NZ), F32),
            pltpu.VMEM((WIDE + 2, 2, 2, NX // 2, NZ), F32),
            pltpu.VMEM((WIDE + 2, 2, 2, NX // 2, NZ), F32),
        ],
    )(spectrum, coefficient)
    solved = exchange(sent, BLOCK)
    sent = call(to_steps, shape(GROUPS, EACH, LOCAL, NZ), [VMEM] * 2)(solved, jnp.asarray(back))
    rows = exchange(sent.reshape(GROUPS * EACH * LOCAL, NZ), TM)
    corrected = call(to_grid, shape(LOCAL, NY, NZ), [VMEM])(rows)
    grid = (LOCAL, 1, NY, NZ)
    return residual.reshape(grid), corrected.reshape(grid)


def solution(mesh):
    fine = Mesh(mesh.devices.reshape(2, 2, 4, 2, 4, 4), AXES)
    big = P(TM, SPACE, None, None)
    plane = P(SPACE, None, None)

    return jax.shard_map(
        local,
        mesh=fine,
        in_specs=(big, big, plane, plane, plane, P(), P()),
        out_specs=(big, big),
        check_vma=False,
    )
```
